512 devices in a mesh: seq: 32 (over y, x, core), dp: 16 (over z).
Axes of the slice: x: 4, y: 4, z: 16, core: 2. Of those that a mesh axis runs over, the one named last changes fastest.
Arguments:
- q_raw: bfloat16 [16, 4096, 4096], P('dp', 'seq'), may hold values from -21 to 21
- k_raw: bfloat16 [16, 4096, 1024], P('dp', 'seq'), may hold values from -21 to 21
- v_raw: bfloat16 [16, 4096, 1024], P('dp', 'seq'), may hold values from -6 to 6
- q_gain: float32 [128], P('dp'), may hold values from 0.5 to 6
- k_gain: float32 [128], P('dp'), may hold values from 0.5 to 6
- key_blocks: int32 [32, 32, 6], P('seq'), may hold values from -1 to 31, as said below
- d_context: bfloat16 [16, 4096, 4096], P('dp', 'seq'), may hold values from -21 to 21
Outputs:
- q_raw_grad: bfloat16 [16, 4096, 4096], P('dp', 'seq')
- k_raw_grad: bfloat16 [16, 4096, 1024], P('dp', 'seq')
- v_grad: bfloat16 [16, 4096, 1024], P('dp', 'seq')
- q_gain_grad: float32 [128], P('dp')
- k_gain_grad: float32 [128], P('dp')
The draws below stay inside these ranges and needn't reach their ends.
Inputs may be any that keep to these rules, and one draw needn't show every extreme that they name: key_blocks[h, b, 0] = b; slots 1 and 2 hold b - 1 and b + 1, or -1 past the ends of the sequence; the next 1 slots hold blocks 0 to 0; the last 2 slots hold drawn blocks, which may repeat earlier slots.
All inputs are finite; a program needn't handle non-finite values.
Results may differ from the reference program's by a relative error of at most 0.017.
The reference program's roundings to bfloat16 on the way count: a program that leaves them out, or rounds other values in their place, can miss the bound.
Values may be sent and summed in bfloat16 or wider, within the bound.
No kernel may reach another device: no remote copies, remote signals or barrier semaphores. Data moves between devices by JAX's collectives and lax.ppermute only.
A program may use at most 64 MiB of HBM per device.

```python
import math
import jax
import jax.numpy as jnp
from jax import lax

HD = 128
HEADS = 32
D = 4096
KVD = 1024
BLK = 128
GLOB = 1
RAND = 2
SEQ = 4096
NB = 32
SEQS = 16


def keys_base(key):
    noise = jax.random.truncated_normal(jax.random.fold_in(key, 11), -5.0, 5.0, (SEQS, SEQ, KVD), jnp.float32)
    return noise


def draw_k_raw(key, part):
    return keys_base(key).astype(jnp.bfloat16)


def draw_q_raw(key, part):
    noise = jax.random.truncated_normal(jax.random.fold_in(key, 12), -5.0, 5.0, (SEQS, SEQ, D), jnp.float32)
    return noise.astype(jnp.bfloat16)


def gain_draw(key, salt):
    low_end = jnp.log(0.5)
    high_end = jnp.log(2.0)
    return jnp.exp(jax.random.uniform(jax.random.fold_in(key, salt), (HD,), jnp.float32, low_end, high_end))


def draw_q_gain(key, part):
    return gain_draw(key, 21)


def draw_k_gain(key, part):
    return gain_draw(key, 22)


def draw_key_blocks(key, part):
    block_ids = jnp.broadcast_to(jnp.arange(NB)[None, :, None], (HEADS, NB, 1))
    before = jnp.where(block_ids > 0, block_ids - 1, -1)
    after = jnp.where(block_ids < NB - 1, block_ids + 1, -1)
    global_ids = jnp.broadcast_to(jnp.arange(GLOB)[None, None, :], (HEADS, NB, GLOB))
    drawn = jax.random.randint(jax.random.fold_in(key, 41), (HEADS, NB, RAND), 0, NB)
    return jnp.concatenate([block_ids, before, after, global_ids, drawn], axis=-1).astype(jnp.int32)


def draw_d_context(key, part):
    noise = jax.random.truncated_normal(jax.random.fold_in(key, 31), -5.0, 5.0, (SEQS, SEQ, D), jnp.float32)
    along = (0.5 + 1.5 * jnp.arange(SEQ) / SEQ)[None, :, None]
    across = (0.5 + jnp.arange(SEQS) / SEQS)[:, None, None]
    return (noise * along * across).astype(jnp.bfloat16)


def steps_of(rng, extent, split, least, largest):
    level = 1.0
    for dim, parts in split:
        steps = jax.random.uniform(jax.random.fold_in(jax.random.fold_in(rng, 6), dim), (parts,), jnp.float32, least / len(split), largest / len(split))
        level = level * jnp.repeat(jnp.exp(steps), extent[dim] // parts).reshape((-1,) + (1,) * (len(extent) - 1 - dim))
    return level


def gaussian(own_key, dims, scale, bound, split=(), held_as=jnp.bfloat16):
    entries = scale * jax.random.normal(own_key, dims, jnp.float32)
    if split:
        entries = entries * steps_of(own_key, dims, split, -0.22, 0.18)
    return jnp.clip(entries, -bound, bound).astype(held_as)


def setup_inputs(seed: int = 0) -> dict:
    keys = jax.random.split(jax.random.key(seed), 8)
    return {
        "q_raw": draw_q_raw(jax.random.fold_in(keys[7], 71), 0),
        "k_raw": draw_k_raw(jax.random.fold_in(keys[7], 71), 0),
        "v_raw": gaussian(keys[2], (SEQS, SEQ, KVD), 1.0, 6.0, ((0, 16), (1, 32))),
        "q_gain": draw_q_gain(jax.random.fold_in(keys[7], 71), 0),
        "k_gain": draw_k_gain(jax.random.fold_in(keys[7], 71), 0),
        "key_blocks": draw_key_blocks(jax.random.fold_in(keys[7], 71), 0),
        "d_context": draw_d_context(jax.random.fold_in(keys[7], 71), 0),
    }


EPSILON = 1e-06

def slot_keep(pattern):
    slot_count = pattern.shape[-1]
    present = pattern >= 0
    same_block = pattern[:, :, None] == pattern[:, None, :]
    earlier = jnp.arange(slot_count)[None, :] < jnp.arange(slot_count)[:, None]
    repeated = jnp.any(same_block & earlier[None, :, :], axis=2)
    return present & jnp.logical_not(repeated)

def norm_rows(raw_rows, gain_vec):
    length_total = raw_rows.shape[0]
    width = gain_vec.shape[0]
    values = raw_rows.astype(jnp.float32).reshape(length_total, -1, width)
    inverse = lax.rsqrt(lax.optimization_barrier(jnp.mean(values * values, axis=-1, keepdims=True)) + EPSILON)
    normed = (values * inverse * gain_vec).astype(jnp.bfloat16).reshape(length_total, -1)
    return (normed, inverse)

def norm_back(raw_rows, inverse, gain_vec, d_normed):
    length_total = raw_rows.shape[0]
    width = gain_vec.shape[0]
    values = raw_rows.astype(jnp.float32).reshape(length_total, -1, width)
    upstream = d_normed.astype(jnp.float32).reshape(length_total, -1, width)
    scaled = gain_vec * upstream
    row_total = lax.optimization_barrier(jnp.sum(scaled * values, axis=-1, keepdims=True))
    d_raw = inverse * scaled - inverse * inverse * inverse * values * row_total / width
    gain_part = lax.optimization_barrier(jnp.sum(upstream * values * inverse, axis=(0, 1)))
    return (d_raw.astype(jnp.bfloat16).reshape(length_total, -1), gain_part)

def rounded(values):
    return lax.optimization_barrier(values.astype(jnp.bfloat16)).astype(jnp.float32)

def softmax_rows(score_matrix, axes):
    row_peak = lax.optimization_barrier(jnp.max(score_matrix, axis=axes, keepdims=True))
    raised = jnp.exp(score_matrix - row_peak)
    return raised / lax.optimization_barrier(jnp.sum(raised, axis=axes, keepdims=True))

def head_pass(q_head, k_head, v_head, d_head, pattern):
    length_total, width_per_head = q_head.shape
    blocks = length_total // BLK
    lead_rows = GLOB * BLK
    logit_scale = 1.0 / math.sqrt(width_per_head)
    keep_slot = slot_keep(pattern)
    picked = jnp.maximum(pattern, 0).astype(jnp.int32)
    top_precision = lax.Precision.HIGHEST
    query_tiles = q_head.astype(jnp.float32).reshape(blocks, BLK, width_per_head)
    k_tiles = k_head.astype(jnp.float32).reshape(blocks, BLK, width_per_head)
    v_tiles = v_head.astype(jnp.float32).reshape(blocks, BLK, width_per_head)
    tile_gradient = d_head.astype(jnp.float32).reshape(blocks, BLK, width_per_head)
    selected_keys = k_tiles[picked]
    selected_values = v_tiles[picked]
    score_matrix = jnp.einsum('vfy,vtwy->vftw', query_tiles, selected_keys, precision=top_precision) * logit_scale
    score_matrix = jnp.where(keep_slot[:, None, :, None], score_matrix, -jnp.inf)
    weights = softmax_rows(score_matrix, (2, 3))
    weight_reduced = rounded(weights)
    sparse_query_row = (jnp.arange(blocks) >= GLOB)[:, None, None, None]
    weight_gradient = jnp.einsum('vfy,vtwy->vftw', tile_gradient, selected_values, precision=top_precision)
    row_delta = lax.optimization_barrier(jnp.sum(weights * weight_gradient, axis=(2, 3), keepdims=True))
    score_gradient = rounded(jnp.where(sparse_query_row, weights * (weight_gradient - row_delta) * logit_scale, 0.0))
    query_sparse = jnp.einsum('lgnw,lnwi->lgi', score_gradient, selected_keys, precision=top_precision).reshape(length_total, width_per_head)
    key_pieces = jnp.einsum('otnc,otj->oncj', score_gradient, query_tiles, precision=top_precision)
    value_pieces = jnp.einsum('otnc,otj->oncj', jnp.where(sparse_query_row, weight_reduced, 0.0), tile_gradient, precision=top_precision)
    one_hot = ((picked[:, :, None] == jnp.arange(blocks)[None, None, :]) & keep_slot[:, :, None]).astype(jnp.float32)
    k_sparse = jnp.einsum('bsn,bskd->nkd', one_hot, key_pieces, precision=top_precision).reshape(length_total, width_per_head)
    v_sparse = jnp.einsum('bsn,bskd->nkd', one_hot, value_pieces, precision=top_precision).reshape(length_total, width_per_head)
    q_lead = q_head[:lead_rows]
    d_lead = d_head[:lead_rows]
    lead_scores = jnp.dot(q_lead, k_head.T, preferred_element_type=jnp.float32) * logit_scale
    lead_weights = softmax_rows(lead_scores, (1,))
    lead_low = lead_weights.astype(jnp.bfloat16)
    lead_dprob = jnp.dot(d_lead, v_head.T, preferred_element_type=jnp.float32)
    lead_delta = lax.optimization_barrier(jnp.sum(lead_weights * lead_dprob, axis=1, keepdims=True))
    lead_dscore = (lead_weights * (lead_dprob - lead_delta) * logit_scale).astype(jnp.bfloat16)
    lead_dq = jnp.dot(lead_dscore, k_head, preferred_element_type=jnp.float32)
    lead_dk = jnp.dot(lead_dscore.T, q_lead, preferred_element_type=jnp.float32)
    lead_dv = jnp.dot(lead_low.T, d_lead, preferred_element_type=jnp.float32)
    d_query = jnp.concatenate([lead_dq, query_sparse[lead_rows:]], axis=0).astype(jnp.bfloat16)
    return (d_query, k_sparse + lead_dk, v_sparse + lead_dv)

def reference(q_raw, k_raw, v_raw, q_gain, k_gain, key_blocks, d_context):
    head_count = key_blocks.shape[0]
    width_per_head = q_gain.shape[0]
    kv_count = k_raw.shape[2] // width_per_head
    group_len = head_count // kv_count

    def one_sequence(inputs):
        q_seq, k_seq, v_seq, d_seq = inputs
        length_total = q_seq.shape[0]
        q_normed, q_inverse = norm_rows(q_seq, q_gain)
        k_normed, k_inverse = norm_rows(k_seq, k_gain)

        def split_heads(block_array):
            return jnp.transpose(block_array.reshape(length_total, -1, width_per_head), (1, 0, 2))

        def widen(block_array):
            return jnp.repeat(split_heads(block_array), group_len, axis=0)

        def one_head(head_items):
            return head_pass(head_items[0], head_items[1], head_items[2], head_items[3], head_items[4])
        results = lax.map(one_head, (split_heads(q_normed), widen(k_normed), widen(v_seq), split_heads(d_seq), key_blocks))
        d_q_normed = jnp.transpose(results[0], (1, 0, 2)).reshape(length_total, head_count * width_per_head)

        def fold_group(head_terms):
            summed = lax.optimization_barrier(jnp.sum(head_terms.reshape(kv_count, group_len, length_total, width_per_head), axis=1)).astype(jnp.bfloat16)
            return jnp.transpose(summed, (1, 0, 2)).reshape(length_total, kv_count * width_per_head)
        d_k_normed = fold_group(results[1])
        v_grad = fold_group(results[2])
        q_grad, q_part = norm_back(q_seq, q_inverse, q_gain, d_q_normed)
        k_grad, k_part = norm_back(k_seq, k_inverse, k_gain, d_k_normed)
        return (q_grad, k_grad, v_grad, q_part, k_part)
    outputs = lax.map(one_sequence, (q_raw, k_raw, v_raw, d_context))
    return (outputs[0], outputs[1], outputs[2], lax.optimization_barrier(jnp.sum(outputs[3], axis=0)), lax.optimization_barrier(jnp.sum(outputs[4], axis=0)))
```

```python
import functools
import math

import jax
import jax.numpy as jnp
from jax import lax
from jax.experimental import pallas as pl
from jax.experimental.pallas import tpu as pltpu
from jax.sharding import PartitionSpec as P

BLK = 128
HD = 128
HALF = BLK // 2
SLOTS = 6
TAIL = 16
EPSILON = 1e-06

F32 = jnp.float32
BF16 = jnp.bfloat16
NT = (((1,), (1,)), ((), ()))
NN = (((1,), (0,)), ((), ()))

VMEM_SPEC = pl.BlockSpec(memory_space=pltpu.VMEM)
SMEM_SPEC = pl.BlockSpec(memory_space=pltpu.SMEM)
ANY_SPEC = pl.BlockSpec(memory_space=pl.ANY)


def run_copies(copies):
    for copy in copies:
        copy.start()
    for copy in copies:
        copy.wait()


def pack_kv_kernel(heads, k_ref, v_ref, out_ref, sems):
    copies = []
    for h in range(heads):
        rows = pl.ds((h % 2) * HALF, HALF)
        cols = pl.ds((h // 4) * HD, HD)
        copies.append(
            pltpu.make_async_copy(k_ref.at[0, rows, cols], out_ref.at[h, pl.ds(0, HALF)], sems.at[2 * h])
        )
        copies.append(
            pltpu.make_async_copy(
                v_ref.at[0, rows, cols], out_ref.at[h, pl.ds(HALF, HALF)], sems.at[2 * h + 1]
            )
        )
    run_copies(copies)


def pack_qd_kernel(heads, q_ref, d_ref, out_ref, sems):
    copies = []
    for h in range(heads):
        cols = pl.ds(h * HD, HD)
        copies.append(
            pltpu.make_async_copy(q_ref.at[0, :, cols], out_ref.at[h, pl.ds(0, BLK)], sems.at[2 * h])
        )
        copies.append(
            pltpu.make_async_copy(d_ref.at[0, :, cols], out_ref.at[h, pl.ds(BLK, BLK)], sems.at[2 * h + 1])
        )
    run_copies(copies)


def inverse_rms(values):
    return lax.rsqrt(jnp.mean(values * values, axis=-1, keepdims=True) + EPSILON)


def prep_kernel(blocks, own_ref, other_ref, gains_ref, kv_ref, kt_ref, khat_ref):
    core = lax.rem(lax.axis_index("seq"), 2)
    own = pl.multiple_of(core * HALF, HALF)
    other = pl.multiple_of((1 - core) * HALF, HALF)
    k_gain = gains_ref[1:2, :]

    def one_block(j, carry):
        for ref, start in ((own_ref, own), (other_ref, other)):
            values = ref[j, 0:HALF, :].astype(F32)
            hat = values * inverse_rms(values)
            khat_ref[j, pl.ds(start, HALF), :] = hat
            kv_ref[j, pl.ds(start, HALF), 0:HD] = (hat * k_gain).astype(BF16)
            kv_ref[j, pl.ds(start, HALF), HD : 2 * HD] = ref[j, HALF:BLK, :]
        kt_ref[j] = kv_ref[j, :, 0:HD].T
        return carry

    lax.fori_loop(0, blocks, one_block, 0, unroll=2)


def attend_kernel(
    blocks, dp_count, pat_ref, gains_ref, qd_ref, kv_ref, kt_ref, khat_ref,
    dq_ref, keep_ref, give_ref, gain_ref, acc_ref, lead_ref,
):
    core = lax.rem(lax.axis_index("seq"), 2)
    q_gain = gains_ref[0:1, :]
    scale = 1.0 / math.sqrt(HD)
    scale2 = scale * math.log2(math.e)
    zeros = jnp.zeros((BLK, HD), BF16)

    def load_query(b):
        q_raw = qd_ref[b, 0:BLK, :].astype(F32)
        d_low = qd_ref[b, BLK : 2 * BLK, :]
        q_inv = inverse_rms(q_raw)
        q_hat = q_raw * q_inv
        q_low = (q_hat * q_gain).astype(BF16)
        pair = jnp.concatenate(
            [jnp.concatenate([q_low, zeros], axis=1), jnp.concatenate([zeros, d_low], axis=1)], axis=0
        )
        return q_raw, q_inv, q_hat, pair

    def store_query(b, q_raw, q_inv, q_hat, dq_t):
        dq = dq_t.T.astype(BF16).astype(F32)
        scaled = q_gain * dq
        total = jnp.sum(scaled * q_raw, axis=-1, keepdims=True)
        grad = q_inv * scaled - q_inv * q_inv * q_inv * q_raw * total / HD
        dq_ref[b] = grad.astype(BF16)
        return jnp.sum((dq * q_hat).reshape(BLK // 8, 8, HD), axis=0)

    q_raw, q_inv, q_hat, pair = load_query(0)
    chunk = 8

    def lead_scores(i, peak):
        rows = kv_ref[pl.ds(i * chunk, chunk)].reshape(chunk * BLK, 2 * HD)
        both = lax.dot_general(rows, pair, NT, preferred_element_type=F32)
        scores = both[:, 0:BLK] * scale2
        start = pl.multiple_of(i * chunk * BLK, chunk * BLK)
        lead_ref[pl.ds(start, chunk * BLK), 0:BLK] = scores
        lead_ref[pl.ds(start, chunk * BLK), BLK : 2 * BLK] = both[:, BLK : 2 * BLK]
        return jnp.maximum(peak, jnp.max(scores.reshape(chunk * BLK // 8, 8, BLK), axis=0))

    peak = lax.fori_loop(0, blocks // chunk, lead_scores, jnp.full((8, BLK), -jnp.inf, F32))
    peak = jnp.max(peak, axis=0, keepdims=True)

    def lead_exp(i, sums):
        start = pl.multiple_of(i * chunk * BLK, chunk * BLK)
        raised = jnp.exp2(lead_ref[pl.ds(start, chunk * BLK), 0:BLK] - peak)
        lead_ref[pl.ds(start, chunk * BLK), 0:BLK] = raised
        product = raised * lead_ref[pl.ds(start, chunk * BLK), BLK : 2 * BLK]
        return (
            sums[0] + jnp.sum(raised.reshape(chunk * BLK // 8, 8, BLK), axis=0),
            sums[1] + jnp.sum(product.reshape(chunk * BLK // 8, 8, BLK), axis=0),
        )

    zero8 = jnp.zeros((8, BLK), F32)
    total, delta = lax.fori_loop(0, blocks // chunk, lead_exp, (zero8, zero8))
    inv_total = 1.0 / jnp.sum(total, axis=0, keepdims=True)
    delta = jnp.sum(delta, axis=0, keepdims=True) * inv_total

    def lead_grad(i, dq_t):
        start = pl.multiple_of(i * chunk * BLK, chunk * BLK)
        weights = lead_ref[pl.ds(start, chunk * BLK), 0:BLK] * inv_total
        d_weights = lead_ref[pl.ds(start, chunk * BLK), BLK : 2 * BLK]
        d_low = (weights * (d_weights - delta) * scale).astype(BF16)
        both = jnp.concatenate([d_low, weights.astype(BF16)], axis=1)
        terms = lax.dot_general(both, pair, NN, preferred_element_type=F32)
        acc_ref[pl.ds(i * chunk, chunk)] = terms.reshape(chunk, BLK, 2 * HD)
        keys = jnp.concatenate([kt_ref[i * chunk + t] for t in range(chunk)], axis=1)
        return dq_t + lax.dot_general(keys, d_low, NN, preferred_element_type=F32)

    dq_t = lax.fori_loop(0, blocks // chunk, lead_grad, jnp.zeros((HD, BLK), F32))
    q_part = store_query(0, q_raw, q_inv, q_hat, dq_t)

    def sparse_block(b, q_part):
        named = [pat_ref[0, b, s] for s in range(SLOTS)]
        index = [jnp.maximum(n, 0) for n in named]
        bias = []
        for s in range(SLOTS):
            kept = named[s] >= 0
            for t in range(s):
                kept = jnp.logical_and(kept, named[s] != named[t])
            bias.append(jnp.where(kept, 0.0, -jnp.inf).astype(F32))
        q_raw, q_inv, q_hat, pair = load_query(b)
        rows = jnp.concatenate([kv_ref[i] for i in index], axis=0)
        both = lax.dot_general(rows, pair, NT, preferred_element_type=F32)
        scores = [both[s * BLK : (s + 1) * BLK, 0:BLK] * scale2 + bias[s] for s in range(SLOTS)]
        d_weights = [both[s * BLK : (s + 1) * BLK, BLK : 2 * BLK] for s in range(SLOTS)]
        peak = functools.reduce(jnp.maximum, scores)
        peak = jnp.max(peak, axis=0, keepdims=True)
        raised = [jnp.exp2(x - peak) for x in scores]
        inv_total = 1.0 / jnp.sum(functools.reduce(jnp.add, raised), axis=0, keepdims=True)
        products = functools.reduce(jnp.add, [x * y for x, y in zip(raised, d_weights)])
        delta = jnp.sum(products, axis=0, keepdims=True) * inv_total
        weights = [x * inv_total for x in raised]
        d_low = [(x * (y - delta) * scale).astype(BF16) for x, y in zip(weights, d_weights)]
        stacked = jnp.concatenate(
            [jnp.concatenate([x, y.astype(BF16)], axis=1) for x, y in zip(d_low, weights)], axis=0
        )
        terms = lax.dot_general(stacked, pair, NN, preferred_element_type=F32)
        keys = jnp.concatenate([kt_ref[i] for i in index], axis=1)
        dq_t = lax.dot_general(keys, jnp.concatenate(d_low, axis=0), NN, preferred_element_type=F32)
        for s in range(SLOTS):
            acc_ref[index[s]] += terms[s * BLK : (s + 1) * BLK]
        return q_part + store_query(b, q_raw, q_inv, q_hat, dq_t)

    q_part = lax.fori_loop(1, blocks, sparse_block, q_part)

    own = pl.multiple_of(core * HALF, HALF)
    other = pl.multiple_of((1 - core) * HALF, HALF)

    def finish(j, k_part):
        keep_ref[j, 0:HALF, :] = acc_ref[j, pl.ds(own, HALF), 0:HD]
        keep_ref[j, HALF:BLK, :] = acc_ref[j, pl.ds(own, HALF), HD : 2 * HD]
        give_ref[j, 0:HALF, :] = acc_ref[j, pl.ds(other, HALF), 0:HD].astype(BF16)
        give_ref[j, HALF:BLK, :] = acc_ref[j, pl.ds(other, HALF), HD : 2 * HD].astype(BF16)
        product = acc_ref[j, :, 0:HD] * khat_ref[j]
        return k_part + jnp.sum(product.reshape(BLK // 8, 8, HD), axis=0)

    k_part = lax.fori_loop(0, blocks, finish, jnp.zeros((8, HD), F32), unroll=2)
    parts = jnp.concatenate(
        [
            jnp.sum(q_part, axis=0, keepdims=True),
            jnp.sum(k_part, axis=0, keepdims=True),
            jnp.zeros((6, HD), F32),
        ],
        axis=0,
    )
    for z in range(dp_count):
        gain_ref[z] = parts


def merge_kernel(blocks, keep_ref, got_ref, gain_ref, out_ref):
    parts = jnp.sum(gain_ref[...], axis=0)
    high = parts.astype(BF16).astype(F32)
    rest = parts - high
    middle = rest.astype(BF16).astype(F32)
    low = rest - middle
    tail = jnp.concatenate(
        [high[0:2], middle[0:2], low[0:2], jnp.zeros((TAIL - 6, HD), F32)], axis=0
    ).astype(BF16)

    def one_block(j, carry):
        out_ref[j, 0:BLK, :] = (keep_ref[j] + got_ref[j].astype(F32)).astype(BF16)
        out_ref[j, BLK : BLK + TAIL, :] = tail
        return carry

    lax.fori_loop(0, blocks, one_block, 0, unroll=4)


def unpack_q_kernel(heads, in_ref, out_ref, sems):
    run_copies(
        [
            pltpu.make_async_copy(in_ref.at[h], out_ref.at[0, :, pl.ds(h * HD, HD)], sems.at[h])
            for h in range(heads)
        ]
    )


def final_kernel(heads, in_ref, k_ref, gains_ref, k_grad_ref, v_grad_ref, gain_ref):
    k_gain = gains_ref[1:2, :]
    for g in range(heads // 4):
        for core in range(2):
            first, second = 4 * g + core, 4 * g + 2 + core
            rows = pl.ds(core * HALF, HALF)
            cols = pl.ds(g * HD, HD)
            d_k = in_ref[first, 0:HALF, :].astype(F32) + in_ref[second, 0:HALF, :].astype(F32)
            d_v = in_ref[first, HALF:BLK, :].astype(F32) + in_ref[second, HALF:BLK, :].astype(F32)
            v_grad_ref[0, rows, cols] = d_v.astype(BF16)
            values = k_ref[0, rows, cols].astype(F32)
            inverse = inverse_rms(values)
            scaled = k_gain * d_k.astype(BF16).astype(F32)
            total = jnp.sum(scaled * values, axis=-1, keepdims=True)
            grad = inverse * scaled - inverse * inverse * inverse * values * total / HD
            k_grad_ref[0, rows, cols] = grad.astype(BF16)
    tails = in_ref[0, BLK : BLK + TAIL, :].astype(F32)
    for s in range(1, heads):
        tails += in_ref[s, BLK : BLK + TAIL, :].astype(F32)
    sums = tails[0:2] + tails[2:4] + tails[4:6]
    shift = lax.rem(HD - 8 * lax.axis_index("dp"), HD)
    gain_ref[...] = pltpu.roll(jnp.concatenate([sums, jnp.zeros((6, HD), F32)], axis=0), shift, 1)


def struct(shape, dtype):
    return jax.ShapeDtypeStruct(shape, dtype)


def shards(heads, dp_count, q_raw, k_raw, v_raw, q_gain, k_gain, key_blocks, d_context):
    blocks = heads
    gain_slices = jnp.concatenate([q_gain[None], k_gain[None]], axis=0)
    gain_all = lax.all_to_all(
        jnp.broadcast_to(gain_slices[None], (dp_count,) + gain_slices.shape), "dp", 0, 0, tiled=True
    )
    gains = jnp.transpose(gain_all, (1, 0, 2)).reshape(2, HD)

    kv_send = pl.pallas_call(
        functools.partial(pack_kv_kernel, heads),
        out_shape=struct((heads, BLK, HD), BF16),
        in_specs=[ANY_SPEC] * 2,
        out_specs=VMEM_SPEC,
        scratch_shapes=[pltpu.SemaphoreType.DMA((2 * heads,))],
        name="pack_kv",
    )(k_raw, v_raw)
    kv_own = lax.all_to_all(kv_send, "seq", 0, 0, tiled=True)
    swap = [(s, s ^ 1) for s in range(heads)]
    kv_other = lax.ppermute(kv_own, "seq", swap)

    qd_send = pl.pallas_call(
        functools.partial(pack_qd_kernel, heads),
        out_shape=struct((heads, 2 * BLK, HD), BF16),
        in_specs=[ANY_SPEC] * 2,
        out_specs=VMEM_SPEC,
        scratch_shapes=[pltpu.SemaphoreType.DMA((2 * heads,))],
        name="pack_qd",
    )(q_raw, d_context)
    qd = lax.all_to_all(qd_send, "seq", 0, 0, tiled=True)

    kv, kt, khat = pl.pallas_call(
        functools.partial(prep_kernel, blocks),
        out_shape=(
            struct((blocks, BLK, 2 * HD), BF16),
            struct((blocks, HD, BLK), BF16),
            struct((blocks, BLK, HD), F32),
        ),
        in_specs=[VMEM_SPEC] * 3,
        out_specs=(VMEM_SPEC,) * 3,
        name="prep",
    )(kv_own, kv_other, gains)

    q_grad_heads, keep, give, gain_terms = pl.pallas_call(
        functools.partial(attend_kernel, blocks, dp_count),
        out_shape=(
            struct((blocks, BLK, HD), BF16),
            struct((blocks, BLK, HD), F32),
            struct((blocks, BLK, HD), BF16),
            struct((dp_count, 8, HD), F32),
        ),
        in_specs=[SMEM_SPEC] + [VMEM_SPEC] * 5,
        out_specs=(VMEM_SPEC,) * 4,
        scratch_shapes=[
            pltpu.VMEM((blocks, BLK, 2 * HD), F32),
            pltpu.VMEM((blocks * BLK, 2 * BLK), F32),
        ],
        name="attend",
    )(key_blocks, gains, qd, kv, kt, khat)

    got = lax.ppermute(give, "seq", swap)
    q_back = lax.all_to_all(q_grad_heads, "seq", 0, 0, tiled=True)
    gain_terms = lax.all_to_all(gain_terms, "dp", 0, 0, tiled=True)

    kv_terms = pl.pallas_call(
        functools.partial(merge_kernel, blocks),
        out_shape=struct((blocks, BLK + TAIL, HD), BF16),
        in_specs=[VMEM_SPEC] * 3,
        out_specs=VMEM_SPEC,
        name="merge",
    )(keep, got, gain_terms)
    kv_back = lax.all_to_all(kv_terms, "seq", 0, 0, tiled=True)

    q_grad = pl.pallas_call(
        functools.partial(unpack_q_kernel, heads),
        out_shape=struct((1, BLK, heads * HD), BF16),
        in_specs=[VMEM_SPEC],
        out_specs=ANY_SPEC,
        scratch_shapes=[pltpu.SemaphoreType.DMA((heads,))],
        name="unpack_q",
    )(q_back)

    k_grad, v_grad, totals = pl.pallas_call(
        functools.partial(final_kernel, heads),
        out_shape=(
            struct(k_raw.shape, BF16),
            struct(v_raw.shape, BF16),
            struct((8, HD), F32),
        ),
        in_specs=[VMEM_SPEC] * 3,
        out_specs=(VMEM_SPEC,) * 3,
        name="final",
    )(kv_back, k_raw, gains)
    width = q_gain.shape[0]
    return (q_grad, k_grad, v_grad, totals[0, :width], totals[1, :width])


def solution(mesh):
    placed = (
        P("dp", "seq", None),
        P("dp", "seq", None),
        P("dp", "seq", None),
        P("dp"),
        P("dp"),
        P("seq", None, None),
        P("dp", "seq", None),
    )
    return jax.shard_map(
        functools.partial(shards, mesh.shape["seq"], mesh.shape["dp"]),
        mesh=mesh,
        in_specs=placed,
        out_specs=(
            P("dp", "seq", None),
            P("dp", "seq", None),
            P("dp", "seq", None),
            P("dp"),
            P("dp"),
        ),
        check_vma=False,
    )
```

```python
import functools
import math

import jax
import jax.numpy as jnp
from jax import lax
from jax.experimental import pallas as pl
from jax.experimental.pallas import tpu as pltpu
from jax.sharding import PartitionSpec as P

BLK = 128
HD = 128
HALF = BLK // 2
SLOTS = 6
PARTS = 8
PACKS = 4
EPSILON = 1e-06

F32 = jnp.float32
BF16 = jnp.bfloat16
NT = (((1,), (1,)), ((), ()))
NN = (((1,), (0,)), ((), ()))

VMEM_SPEC = pl.BlockSpec(memory_space=pltpu.VMEM)
SMEM_SPEC = pl.BlockSpec(memory_space=pltpu.SMEM)
HBM_SPEC = pl.BlockSpec(memory_space=pltpu.HBM)


def run_copies(copies):
    for copy in copies:
        copy.start()
    for copy in copies:
        copy.wait()


def pack_kernel(heads, q_ref, d_ref, k_ref, v_ref, out_any, held_ref, sems, out_sems):
    copies = []
    for h in range(heads):
        rows = pl.ds((h % 2) * HALF, HALF)
        wide = pl.ds(h * HD, HD)
        cols = pl.ds((h // 4) * HD, HD)
        parts = (
            (q_ref.at[0, :, wide], 0, BLK),
            (d_ref.at[0, :, wide], BLK, BLK),
            (k_ref.at[0, rows, cols], 2 * BLK, HALF),
            (v_ref.at[0, rows, cols], 2 * BLK + HALF, HALF),
        )
        copies.append(
            [
                pltpu.make_async_copy(source, held_ref.at[h, pl.ds(first, count)], sems.at[4 * h + n])
                for n, (source, first, count) in enumerate(parts)
            ]
        )
    for group in copies:
        for copy in group:
            copy.start()
    step = heads // PACKS
    outs = []
    for n in range(PACKS):
        for group in copies[n * step : (n + 1) * step]:
            for copy in group:
                copy.wait()
        chunk = pl.ds(n * step, step)
        outs.append(pltpu.make_async_copy(held_ref.at[chunk], out_any.at[chunk], out_sems.at[n]))
        outs[-1].start()
    for copy in outs:
        copy.wait()


def inverse_rms(values):
    return lax.rsqrt(jnp.mean(values * values, axis=-1, keepdims=True) + EPSILON)


def rows_sum(values):
    return jnp.sum(values.reshape(values.shape[0] // 8, 8, values.shape[1]), axis=0)


def named_blocks(pat_ref, b):
    named = [pat_ref[0, b, s] for s in range(SLOTS)]
    return named, [jnp.maximum(n, 0) for n in named]


SCALE = 1.0 / math.sqrt(HD)
SCALE2 = SCALE * math.log2(math.e)
CHUNK = 8
GROUPS = [list(range(s, s + 2)) for s in range(0, SLOTS, 2)]


def attend_kernel(
    blocks, pat_ref, gains_ref, got_ref, other_ref,
    send_any, keep_ref, give_ref, parts_ref,
    dq_ref, acc_ref, lead_ref, lead_dq_ref, kv_ref, kt_ref, khat_ref, qn_ref,
    s0, s1, g0, g1, x0, x1, peak_ref, sem,
):
    s_refs, g_refs, x_refs = (s0, s1), (g0, g1), (x0, x1)
    q_gain = gains_ref[0:1, :]
    k_gain = gains_ref[1:2, :]
    zeros = jnp.zeros((BLK, HD), BF16)
    own_k, own_v = pl.ds(2 * BLK, HALF), pl.ds(2 * BLK + HALF, HALF)

    def normalise(j, carry):
        k_raw = jnp.concatenate([got_ref[j, own_k, :], other_ref[j, 0:HALF, :]], axis=0).astype(F32)
        k_hat = k_raw * inverse_rms(k_raw)
        k_low = (k_hat * k_gain).astype(BF16)
        q_raw = got_ref[j, 0:BLK, :].astype(F32)
        q_low = (q_raw * inverse_rms(q_raw) * q_gain).astype(BF16)
        khat_ref[j] = k_hat
        kv_ref[j, :, 0:HD] = k_low
        kv_ref[j, :, HD : 2 * HD] = jnp.concatenate([got_ref[j, own_v, :], other_ref[j, HALF:BLK, :]], axis=0)
        kt_ref[j] = k_low.T
        qn_ref[j] = q_low
        return carry

    lax.fori_loop(0, blocks, normalise, 0, unroll=4)

    def pair_of(b):
        d_low = got_ref[b, BLK : 2 * BLK, :]
        return jnp.concatenate(
            [jnp.concatenate([qn_ref[b], zeros], axis=1), jnp.concatenate([zeros, d_low], axis=1)], axis=0
        )

    def slot_rows(s):
        return pl.ds(s * BLK, BLK)

    pair = pair_of(0)

    def chunk_rows(i):
        return pl.ds(pl.multiple_of(i * CHUNK * BLK, CHUNK * BLK), CHUNK * BLK)

    def lead_scores(i, peak):
        rows = kv_ref[pl.ds(i * CHUNK, CHUNK)].reshape(CHUNK * BLK, 2 * HD)
        both = lax.dot_general(rows, pair, NT, preferred_element_type=F32)
        lead_ref[chunk_rows(i), :] = both
        return jnp.maximum(peak, jnp.max(both[:, 0:BLK].reshape(CHUNK * BLK // 8, 8, BLK), axis=0))

    peak = lax.fori_loop(0, blocks // CHUNK, lead_scores, jnp.full((8, BLK), -jnp.inf, F32))
    peak = jnp.max(peak, axis=0, keepdims=True) * SCALE2

    def lead_exp(i, sums):
        raised = jnp.exp2(lead_ref[chunk_rows(i), 0:BLK] * SCALE2 - peak)
        lead_ref[chunk_rows(i), 0:BLK] = raised
        product = raised * lead_ref[chunk_rows(i), BLK : 2 * BLK]
        return sums[0] + rows_sum(raised), sums[1] + rows_sum(product)

    zero8 = jnp.zeros((8, BLK), F32)
    total, delta = lax.fori_loop(0, blocks // CHUNK, lead_exp, (zero8, zero8))
    lead_inv = 1.0 / jnp.sum(total, axis=0, keepdims=True)
    lead_delta = jnp.sum(delta, axis=0, keepdims=True) * lead_inv

    def lead_grad(i, dq_t):
        weights = lead_ref[chunk_rows(i), 0:BLK] * lead_inv
        d_weights = lead_ref[chunk_rows(i), BLK : 2 * BLK]
        d_low = (weights * (d_weights - lead_delta) * SCALE).astype(BF16)
        both = jnp.concatenate([d_low, weights.astype(BF16)], axis=1)
        terms = lax.dot_general(both, pair, NN, preferred_element_type=F32)
        acc_ref[pl.ds(i * CHUNK, CHUNK)] = terms.reshape(CHUNK, BLK, 2 * HD)
        keys = jnp.concatenate([kt_ref[i * CHUNK + t] for t in range(CHUNK)], axis=1)
        return dq_t + lax.dot_general(keys, d_low, NN, preferred_element_type=F32)

    lead_dq_ref[...] = lax.fori_loop(0, blocks // CHUNK, lead_grad, jnp.zeros((HD, BLK), F32))

    def scores_slots(b, side, slots, pair, peak):
        index = named_blocks(pat_ref, b)[1]
        rows = jnp.concatenate([kv_ref[index[s]] for s in slots], axis=0)
        both = lax.dot_general(rows, pair, NT, preferred_element_type=F32)
        span = pl.ds(slots[0] * BLK, len(slots) * BLK)
        s_refs[side][span, :] = both[:, 0:BLK]
        g_refs[side][span, :] = both[:, BLK : 2 * BLK]
        top = jnp.max(both[:, 0:BLK].reshape(len(slots) * BLK // 8, 8, BLK), axis=0)
        return top if peak is None else jnp.maximum(peak, top)

    def exp_slot(b, side, s, peak, sums):
        named = named_blocks(pat_ref, b)[0]
        kept = named[s] >= 0
        for t in range(s):
            kept = jnp.logical_and(kept, named[s] != named[t])
        floor = peak + jnp.where(kept, 0.0, jnp.inf).astype(F32)
        raised = jnp.exp2(s_refs[side][slot_rows(s), :] * SCALE2 - floor)
        s_refs[side][slot_rows(s), :] = raised
        product = raised * g_refs[side][slot_rows(s), :]
        return sums[0] + rows_sum(raised), sums[1] + rows_sum(product)

    def grads_slots(side, slots, pair, inv_total, inv_scaled, delta):
        span = pl.ds(slots[0] * BLK, len(slots) * BLK)
        raised = s_refs[side][span, :]
        d_low = (raised * inv_scaled * (g_refs[side][span, :] - delta)).astype(BF16)
        x_refs[side][span, :] = d_low
        both = jnp.concatenate([d_low, (raised * inv_total).astype(BF16)], axis=1)
        return lax.dot_general(both, pair, NN, preferred_element_type=F32)

    def query_product(b, side):
        index = named_blocks(pat_ref, b)[1]
        keys = jnp.concatenate([kt_ref[i] for i in index], axis=1)
        return lax.dot_general(keys, x_refs[side][...], NN, preferred_element_type=F32)

    def query_grad(b, dq_t, q_part):
        dq = dq_t.T.astype(BF16).astype(F32)
        q_raw = got_ref[b, 0:BLK, :].astype(F32)
        q_inv = inverse_rms(q_raw)
        q_hat = q_raw * q_inv
        scaled = q_gain * dq
        mean = jnp.mean(scaled * q_hat, axis=-1, keepdims=True)
        dq_ref[b] = (q_inv * (scaled - q_hat * mean)).astype(BF16)
        return q_part + rows_sum(dq * q_hat)

    def step(b, side, q_part, ahead=True, behind=True):
        peak = peak_ref[side, 0:1, :] * SCALE2
        sums = (zero8, zero8)
        pair = pair_of(b + 1) if ahead else None
        top = None
        dq_t = query_product(b - 1, 1 - side) if behind else None
        for slots in GROUPS:
            if ahead:
                top = scores_slots(b + 1, 1 - side, slots, pair, top)
            for s in slots:
                sums = exp_slot(b, side, s, peak, sums)
        if ahead:
            peak_ref[1 - side, 0:1, :] = jnp.max(top, axis=0, keepdims=True)
        inv_total = 1.0 / jnp.sum(sums[0], axis=0, keepdims=True)
        delta = jnp.sum(sums[1], axis=0, keepdims=True) * inv_total
        pair = pair_of(b)
        index = named_blocks(pat_ref, b)[1]
        for slots in GROUPS:
            terms = grads_slots(side, slots, pair, inv_total, inv_total * SCALE, delta)
            for n, s in enumerate(slots):
                acc_ref[index[s]] += terms[n * BLK : (n + 1) * BLK]
        return query_grad(b - 1, dq_t, q_part) if behind else q_part

    x0[...] = jnp.zeros_like(x0)
    pair = pair_of(1)
    top = None
    for slots in GROUPS:
        top = scores_slots(1, 1, slots, pair, top)
    peak_ref[1, 0:1, :] = jnp.max(top, axis=0, keepdims=True)

    def two_steps(i, q_part):
        q_part = step(2 * i + 1, 1, q_part)
        return step(2 * i + 2, 0, q_part)

    q_part = lax.fori_loop(0, blocks // 2 - 1, two_steps, zero8)
    q_part = step(blocks - 1, 1, q_part, ahead=False)
    q_part = query_grad(blocks - 1, query_product(blocks - 1, 1), q_part)
    q_part = query_grad(0, lead_dq_ref[...], q_part)
    dq_copy = pltpu.make_async_copy(dq_ref, send_any.at[:, pl.ds(0, BLK)], sem)
    dq_copy.start()

    def finish(j, k_part):
        keep_ref[j, 0:HALF, :] = acc_ref[j, 0:HALF, 0:HD]
        keep_ref[j, HALF:BLK, :] = acc_ref[j, 0:HALF, HD : 2 * HD]
        give_ref[j, 0:HALF, :] = acc_ref[j, HALF:BLK, 0:HD].astype(BF16)
        give_ref[j, HALF:BLK, :] = acc_ref[j, HALF:BLK, HD : 2 * HD].astype(BF16)
        return k_part + rows_sum(acc_ref[j, :, 0:HD] * khat_ref[j])

    k_part = lax.fori_loop(0, blocks, finish, zero8, unroll=2)
    parts = jnp.concatenate(
        [
            jnp.sum(q_part, axis=0, keepdims=True),
            jnp.sum(k_part, axis=0, keepdims=True),
            jnp.zeros((PARTS - 2, HD), F32),
        ],
        axis=0,
    )
    for j in range(blocks):
        parts_ref[j] = parts
    dq_copy.wait()


def merge_kernel(blocks, keep_ref, got_ref, send_any, out_any, sum_ref, sem):
    def one_block(j, carry):
        sum_ref[j] = (keep_ref[j] + got_ref[j].astype(F32)).astype(BF16)
        return carry

    lax.fori_loop(0, blocks, one_block, 0, unroll=4)
    run_copies([pltpu.make_async_copy(sum_ref, out_any.at[:, pl.ds(BLK, BLK)], sem)])


def parts_sum_kernel(in_ref, out_ref):
    out_ref[...] = jnp.sum(in_ref[...], axis=0)[0:2]


def final_kernel(heads, in_ref, k_ref, gains_ref, q_grad_any, k_grad_ref, v_grad_ref, sems):
    copies = [
        pltpu.make_async_copy(in_ref.at[h, pl.ds(0, BLK)], q_grad_any.at[0, :, pl.ds(h * HD, HD)], sems.at[h])
        for h in range(heads)
    ]
    for copy in copies:
        copy.start()
    k_gain = gains_ref[1:2, :]
    for g in range(heads // 4):
        for core in range(2):
            first, second = 4 * g + core, 4 * g + 2 + core
            rows = pl.ds(core * HALF, HALF)
            cols = pl.ds(g * HD, HD)
            both = in_ref[first, BLK : 2 * BLK, :].astype(F32) + in_ref[second, BLK : 2 * BLK, :].astype(F32)
            v_grad_ref[0, rows, cols] = both[HALF:BLK].astype(BF16)
            values = k_ref[0, rows, cols].astype(F32)
            inverse = inverse_rms(values)
            scaled = k_gain * both[0:HALF].astype(BF16).astype(F32)
            total = jnp.sum(scaled * values, axis=-1, keepdims=True)
            grad = inverse * scaled - inverse * inverse * inverse * values * total / HD
            k_grad_ref[0, rows, cols] = grad.astype(BF16)
    for copy in copies:
        copy.wait()


def dp_step(values, step, dp_count):
    if step >= dp_count:
        return values
    return values + lax.ppermute(values, "dp", [(z, z ^ step) for z in range(dp_count)])


def struct(shape, dtype):
    return jax.ShapeDtypeStruct(shape, dtype)


def call(kernel, name, ins, outs, scratch=(), mib=12, aliases={}):
    return pl.pallas_call(
        kernel,
        out_shape=tuple(array for array, spec in outs),
        in_specs=list(ins),
        out_specs=tuple(spec for array, spec in outs),
        scratch_shapes=list(scratch),
        input_output_aliases=aliases,
        compiler_params=pltpu.CompilerParams(vmem_limit_bytes=mib << 20),
        name=name,
    )


def shards(heads, dp_count, q_raw, k_raw, v_raw, q_gain, k_gain, key_blocks, d_context):
    blocks = heads
    swap = [(s, s ^ 1) for s in range(heads)]
    mine = lax.broadcasted_iota(jnp.int32, (2, HD), 1) // (HD // dp_count) == lax.axis_index("dp")
    spread = jnp.concatenate([jnp.tile(q_gain, dp_count)[None], jnp.tile(k_gain, dp_count)[None]], axis=0)
    gains = jnp.where(mine, spread, 0.0)

    (sent,) = call(
        functools.partial(pack_kernel, heads),
        "pack",
        [HBM_SPEC] * 4,
        [(pltpu.HBM((heads, 3 * BLK, HD), BF16), HBM_SPEC)],
        [
            pltpu.VMEM((heads, 3 * BLK, HD), BF16),
            pltpu.SemaphoreType.DMA((4 * heads,)),
            pltpu.SemaphoreType.DMA((PACKS,)),
        ],
    )(*[pltpu.with_memory_space_constraint(x, pltpu.HBM) for x in (q_raw, d_context, k_raw, v_raw)])
    arrived = lax.all_to_all(sent, "seq", 0, 0, tiled=True)
    for step in (8, 4, 2, 1):
        gains = dp_step(gains, step, dp_count)
    arrived, gains = lax.optimization_barrier((arrived, gains))
    other = lax.ppermute(arrived[:, 2 * BLK :], "seq", swap)

    send, keep, give, parts = call(
        functools.partial(attend_kernel, blocks),
        "attend",
        [SMEM_SPEC] + [VMEM_SPEC] * 3,
        [
            (pltpu.HBM((blocks, 2 * BLK, HD), BF16), HBM_SPEC),
            (pltpu.HBM((blocks, BLK, HD), F32), VMEM_SPEC),
            (pltpu.HBM((blocks, BLK, HD), BF16), VMEM_SPEC),
            (struct((blocks, PARTS, HD), F32), VMEM_SPEC),
        ],
        [
            pltpu.VMEM((blocks, BLK, HD), BF16),
            pltpu.VMEM((blocks, BLK, 2 * HD), F32),
            pltpu.VMEM((blocks * BLK, 2 * BLK), F32),
            pltpu.VMEM((HD, BLK), F32),
            pltpu.VMEM((blocks, BLK, 2 * HD), BF16),
            pltpu.VMEM((blocks, HD, BLK), BF16),
            pltpu.VMEM((blocks, BLK, HD), F32),
            pltpu.VMEM((blocks, BLK, HD), BF16),
        ]
        + [pltpu.VMEM((SLOTS * BLK, BLK), F32)] * 4
        + [pltpu.VMEM((SLOTS * BLK, BLK), BF16)] * 2
        + [pltpu.VMEM((2, 8, BLK), F32), pltpu.SemaphoreType.DMA],
        mib=40,
    )(key_blocks, gains, arrived, other)

    parts = lax.all_to_all(parts, "seq", 0, 0, tiled=True)
    got = lax.ppermute(give, "seq", swap)
    (send,) = call(
        functools.partial(merge_kernel, blocks),
        "merge",
        [VMEM_SPEC] * 2 + [HBM_SPEC],
        [(pltpu.HBM(send.shape, BF16), HBM_SPEC)],
        [pltpu.VMEM((blocks, BLK, HD), BF16), pltpu.SemaphoreType.DMA],
        aliases={2: 0},
    )(keep, got, send)
    back = lax.all_to_all(send, "seq", 0, 0, tiled=True)

    (totals,) = call(parts_sum_kernel, "parts_sum", [VMEM_SPEC], [(struct((2, HD), F32), VMEM_SPEC)])(parts)
    for step in (1, 2, 4, 8):
        totals = dp_step(totals, step, dp_count)
    width = q_gain.shape[0]
    totals = lax.dynamic_slice_in_dim(totals, lax.axis_index("dp") * width, width, axis=1)

    q_grad, k_grad, v_grad = call(
        functools.partial(final_kernel, heads),
        "final",
        [VMEM_SPEC] * 3,
        [
            (struct(q_raw.shape, BF16), HBM_SPEC),
            (struct(k_raw.shape, BF16), VMEM_SPEC),
            (struct(v_raw.shape, BF16), VMEM_SPEC),
        ],
        [pltpu.SemaphoreType.DMA((heads,))],
    )(back, k_raw, gains)
    return (q_grad, k_grad, v_grad, totals[0], totals[1])


def solution(mesh):
    placed = (
        P("dp", "seq", None),
        P("dp", "seq", None),
        P("dp", "seq", None),
        P("dp"),
        P("dp"),
        P("seq", None, None),
        P("dp", "seq", None),
    )
    return jax.shard_map(
        functools.partial(shards, mesh.shape["seq"], mesh.shape["dp"]),
        mesh=mesh,
        in_specs=placed,
        out_specs=(
            P("dp", "seq", None),
            P("dp", "seq", None),
            P("dp", "seq", None),
            P("dp"),
            P("dp"),
        ),
        check_vma=False,
    )
```

```python
import functools
import math

import jax
import jax.numpy as jnp
from jax import lax
from jax.experimental import pallas as pl
from jax.experimental.pallas import tpu as pltpu
from jax.sharding import PartitionSpec as P

BLK = 128
HD = 128
HALF = BLK // 2
SLOTS = 6
PARTS = 8
PACKS = 4
OUTS = 4
EPSILON = 1e-06

F32 = jnp.float32
BF16 = jnp.bfloat16
NT = (((1,), (1,)), ((), ()))
NN = (((1,), (0,)), ((), ()))

VMEM_SPEC = pl.BlockSpec(memory_space=pltpu.VMEM)
SMEM_SPEC = pl.BlockSpec(memory_space=pltpu.SMEM)
HBM_SPEC = pl.BlockSpec(memory_space=pltpu.HBM)


def run_copies(copies):
    for copy in copies:
        copy.start()
    for copy in copies:
        copy.wait()


def pack_kernel(heads, q_any, d_any, k_any, v_any, out_any, q_ref, d_ref, k_ref, v_ref, out_ref, sems, out_sems):
    step = heads // PACKS
    loads = []
    for n in range(PACKS):
        wide = pl.ds(n * step * HD, step * HD)
        cols = pl.ds(n * (step // 4) * HD, (step // 4) * HD)
        arrays = ((q_any, q_ref, wide), (d_any, d_ref, wide), (k_any, k_ref, cols), (v_any, v_ref, cols))
        loads.append(
            [
                pltpu.make_async_copy(source.at[0, :, span], held.at[:, span], sems.at[4 * n + i])
                for i, (source, held, span) in enumerate(arrays)
            ]
        )
    for group in loads:
        for copy in group:
            copy.start()
    outs = []
    for n in range(PACKS):
        for copy in loads[n]:
            copy.wait()
        for h in range(n * step, (n + 1) * step):
            half = (h % 2) * HALF
            rows = slice(half, half + HALF)
            wide = slice(h * HD, (h + 1) * HD)
            cols = slice((h // 4) * HD, (h // 4 + 1) * HD)
            out_ref[h, 0:BLK, :] = q_ref[:, wide]
            out_ref[h, BLK : 2 * BLK, :] = d_ref[:, wide]
            out_ref[h, 2 * BLK : 2 * BLK + HALF, :] = k_ref[rows, cols]
            out_ref[h, 2 * BLK + HALF : 3 * BLK, :] = v_ref[rows, cols]
        chunk = pl.ds(n * step, step)
        outs.append(pltpu.make_async_copy(out_ref.at[chunk], out_any.at[chunk], out_sems.at[n]))
        outs[-1].start()
    for copy in outs:
        copy.wait()


def inverse_rms(values):
    return lax.rsqrt(jnp.mean(values * values, axis=-1, keepdims=True) + EPSILON)


def rows_sum(values):
    return jnp.sum(values.reshape(values.shape[0] // 8, 8, values.shape[1]), axis=0)


def named_blocks(pat_ref, b):
    named = [pat_ref[0, b, s] for s in range(SLOTS)]
    return named, [jnp.maximum(n, 0) for n in named]


SCALE = 1.0 / math.sqrt(HD)
SCALE2 = SCALE * math.log2(math.e)
CHUNK = 8
GROUPS = [list(range(s, s + 2)) for s in range(0, SLOTS, 2)]


def attend_kernel(
    blocks, pat_ref, gains_ref, got_ref, other_ref,
    send_any, keep_any, give_any, parts_ref,
    dq_ref, keep_ref, give_ref, acc_ref, lead_ref, lead_dq_ref, kv_ref, kt_ref, khat_ref, qn_ref,
    s0, s1, g0, g1, x0, x1, peak_ref, sem, give_sems, keep_sems,
):
    s_refs, g_refs, x_refs = (s0, s1), (g0, g1), (x0, x1)
    q_gain = gains_ref[0:1, :]
    k_gain = gains_ref[1:2, :]
    zeros = jnp.zeros((BLK, HD), BF16)
    own_k, own_v = pl.ds(2 * BLK, HALF), pl.ds(2 * BLK + HALF, HALF)

    def normalise(j, carry):
        k_raw = jnp.concatenate([got_ref[j, own_k, :], other_ref[j, 0:HALF, :]], axis=0).astype(F32)
        k_hat = k_raw * inverse_rms(k_raw)
        k_low = (k_hat * k_gain).astype(BF16)
        q_raw = got_ref[j, 0:BLK, :].astype(F32)
        q_low = (q_raw * inverse_rms(q_raw) * q_gain).astype(BF16)
        khat_ref[j] = k_hat
        kv_ref[j, :, 0:HD] = k_low
        kv_ref[j, :, HD : 2 * HD] = jnp.concatenate([got_ref[j, own_v, :], other_ref[j, HALF:BLK, :]], axis=0)
        kt_ref[j] = k_low.T
        qn_ref[j] = q_low
        return carry

    lax.fori_loop(0, blocks, normalise, 0, unroll=4)

    def pair_of(b):
        d_low = got_ref[b, BLK : 2 * BLK, :]
        return jnp.concatenate(
            [jnp.concatenate([qn_ref[b], zeros], axis=1), jnp.concatenate([zeros, d_low], axis=1)], axis=0
        )

    def slot_rows(s):
        return pl.ds(s * BLK, BLK)

    pair = pair_of(0)

    def chunk_rows(i):
        return pl.ds(pl.multiple_of(i * CHUNK * BLK, CHUNK * BLK), CHUNK * BLK)

    def lead_scores(i, peak):
        rows = kv_ref[pl.ds(i * CHUNK, CHUNK)].reshape(CHUNK * BLK, 2 * HD)
        both = lax.dot_general(rows, pair, NT, preferred_element_type=F32)
        lead_ref[chunk_rows(i), :] = both
        return jnp.maximum(peak, jnp.max(both[:, 0:BLK].reshape(CHUNK * BLK // 8, 8, BLK), axis=0))

    peak = lax.fori_loop(0, blocks // CHUNK, lead_scores, jnp.full((8, BLK), -jnp.inf, F32))
    peak = jnp.max(peak, axis=0, keepdims=True) * SCALE2

    def lead_exp(i, sums):
        raised = jnp.exp2(lead_ref[chunk_rows(i), 0:BLK] * SCALE2 - peak)
        lead_ref[chunk_rows(i), 0:BLK] = raised
        product = raised * lead_ref[chunk_rows(i), BLK : 2 * BLK]
        return sums[0] + rows_sum(raised), sums[1] + rows_sum(product)

    zero8 = jnp.zeros((8, BLK), F32)
    total, delta = lax.fori_loop(0, blocks // CHUNK, lead_exp, (zero8, zero8))
    lead_inv = 1.0 / jnp.sum(total, axis=0, keepdims=True)
    lead_delta = jnp.sum(delta, axis=0, keepdims=True) * lead_inv

    def lead_grad(i, dq_t):
        weights = lead_ref[chunk_rows(i), 0:BLK] * lead_inv
        d_weights = lead_ref[chunk_rows(i), BLK : 2 * BLK]
        d_low = (weights * (d_weights - lead_delta) * SCALE).astype(BF16)
        both = jnp.concatenate([d_low, weights.astype(BF16)], axis=1)
        terms = lax.dot_general(both, pair, NN, preferred_element_type=F32)
        acc_ref[pl.ds(i * CHUNK, CHUNK)] = terms.reshape(CHUNK, BLK, 2 * HD)
        keys = jnp.concatenate([kt_ref[i * CHUNK + t] for t in range(CHUNK)], axis=1)
        return dq_t + lax.dot_general(keys, d_low, NN, preferred_element_type=F32)

    lead_dq_ref[...] = lax.fori_loop(0, blocks // CHUNK, lead_grad, jnp.zeros((HD, BLK), F32))

    def scores_slots(b, side, slots, pair, peak):
        index = named_blocks(pat_ref, b)[1]
        rows = jnp.concatenate([kv_ref[index[s]] for s in slots], axis=0)
        both = lax.dot_general(rows, pair, NT, preferred_element_type=F32)
        span = pl.ds(slots[0] * BLK, len(slots) * BLK)
        s_refs[side][span, :] = both[:, 0:BLK]
        g_refs[side][span, :] = both[:, BLK : 2 * BLK]
        top = jnp.max(both[:, 0:BLK].reshape(len(slots) * BLK // 8, 8, BLK), axis=0)
        return top if peak is None else jnp.maximum(peak, top)

    def exp_slot(b, side, s, peak, sums):
        named = named_blocks(pat_ref, b)[0]
        kept = named[s] >= 0
        for t in range(s):
            kept = jnp.logical_and(kept, named[s] != named[t])
        floor = peak + jnp.where(kept, 0.0, jnp.inf).astype(F32)
        raised = jnp.exp2(s_refs[side][slot_rows(s), :] * SCALE2 - floor)
        s_refs[side][slot_rows(s), :] = raised
        product = raised * g_refs[side][slot_rows(s), :]
        return sums[0] + rows_sum(raised), sums[1] + rows_sum(product)

    def grads_slots(side, slots, pair, inv_total, inv_scaled, delta):
        span = pl.ds(slots[0] * BLK, len(slots) * BLK)
        raised = s_refs[side][span, :]
        d_low = (raised * inv_scaled * (g_refs[side][span, :] - delta)).astype(BF16)
        x_refs[side][span, :] = d_low
        both = jnp.concatenate([d_low, (raised * inv_total).astype(BF16)], axis=1)
        return lax.dot_general(both, pair, NN, preferred_element_type=F32)

    def query_product(b, side):
        index = named_blocks(pat_ref, b)[1]
        keys = jnp.concatenate([kt_ref[i] for i in index], axis=1)
        return lax.dot_general(keys, x_refs[side][...], NN, preferred_element_type=F32)

    def query_grad(b, dq_t, q_part):
        dq = dq_t.T.astype(BF16).astype(F32)
        q_raw = got_ref[b, 0:BLK, :].astype(F32)
        q_inv = inverse_rms(q_raw)
        q_hat = q_raw * q_inv
        scaled = q_gain * dq
        mean = jnp.mean(scaled * q_hat, axis=-1, keepdims=True)
        dq_ref[b] = (q_inv * (scaled - q_hat * mean)).astype(BF16)
        return q_part + rows_sum(dq * q_hat)

    def step(b, side, q_part, ahead=True, behind=True):
        peak = peak_ref[side, 0:1, :] * SCALE2
        sums = (zero8, zero8)
        pair = pair_of(b + 1) if ahead else None
        top = None
        dq_t = query_product(b - 1, 1 - side) if behind else None
        for slots in GROUPS:
            if ahead:
                top = scores_slots(b + 1, 1 - side, slots, pair, top)
            for s in slots:
                sums = exp_slot(b, side, s, peak, sums)
        if ahead:
            peak_ref[1 - side, 0:1, :] = jnp.max(top, axis=0, keepdims=True)
        inv_total = 1.0 / jnp.sum(sums[0], axis=0, keepdims=True)
        delta = jnp.sum(sums[1], axis=0, keepdims=True) * inv_total
        pair = pair_of(b)
        index = named_blocks(pat_ref, b)[1]
        for slots in GROUPS:
            terms = grads_slots(side, slots, pair, inv_total, inv_total * SCALE, delta)
            for n, s in enumerate(slots):
                acc_ref[index[s]] += terms[n * BLK : (n + 1) * BLK]
        return query_grad(b - 1, dq_t, q_part) if behind else q_part

    x0[...] = jnp.zeros_like(x0)
    pair = pair_of(1)
    top = None
    for slots in GROUPS:
        top = scores_slots(1, 1, slots, pair, top)
    peak_ref[1, 0:1, :] = jnp.max(top, axis=0, keepdims=True)

    def two_steps(i, q_part):
        q_part = step(2 * i + 1, 1, q_part)
        return step(2 * i + 2, 0, q_part)

    q_part = lax.fori_loop(0, blocks // 2 - 1, two_steps, zero8)
    q_part = step(blocks - 1, 1, q_part, ahead=False)
    q_part = query_grad(blocks - 1, query_product(blocks - 1, 1), q_part)
    q_part = query_grad(0, lead_dq_ref[...], q_part)
    dq_copy = pltpu.make_async_copy(dq_ref, send_any.at[:, pl.ds(0, BLK)], sem)
    dq_copy.start()

    def finish(j, k_part):
        for half, ref in ((0, keep_ref), (HALF, give_ref)):
            rows = pl.ds(half, HALF)
            ref[j, 0:HALF, :] = acc_ref[j, rows, 0:HD].astype(BF16)
            ref[j, HALF:BLK, :] = acc_ref[j, rows, HD : 2 * HD].astype(BF16)
        return k_part + rows_sum(acc_ref[j, :, 0:HD] * khat_ref[j])

    k_part = zero8
    step_blocks = blocks // OUTS
    out_copies = []
    for n in range(OUTS):
        k_part = lax.fori_loop(n * step_blocks, (n + 1) * step_blocks, finish, k_part, unroll=2)
        chunk = pl.ds(n * step_blocks, step_blocks)
        for ref, out, copy_sems in ((give_ref, give_any, give_sems), (keep_ref, keep_any, keep_sems)):
            out_copies.append(pltpu.make_async_copy(ref.at[chunk], out.at[chunk], copy_sems.at[n]))
            out_copies[-1].start()
    parts = jnp.concatenate(
        [
            jnp.sum(q_part, axis=0, keepdims=True),
            jnp.sum(k_part, axis=0, keepdims=True),
            jnp.zeros((PARTS - 2, HD), F32),
        ],
        axis=0,
    )
    for j in range(blocks):
        parts_ref[j] = parts
    dq_copy.wait()
    for copy in out_copies:
        copy.wait()


def merge_kernel(blocks, keep_ref, got_ref, send_any, out_any, sum_ref, sem):
    def one_block(j, carry):
        sum_ref[j] = (keep_ref[j].astype(F32) + got_ref[j].astype(F32)).astype(BF16)
        return carry

    lax.fori_loop(0, blocks, one_block, 0, unroll=4)
    run_copies([pltpu.make_async_copy(sum_ref, out_any.at[:, pl.ds(BLK, BLK)], sem)])


def parts_sum_kernel(in_ref, out_ref):
    out_ref[...] = jnp.sum(in_ref[...], axis=0)[0:2]


def final_kernel(heads, in_ref, k_ref, gains_ref, q_grad_any, k_grad_ref, v_grad_ref, sems):
    copies = [
        pltpu.make_async_copy(in_ref.at[h, pl.ds(0, BLK)], q_grad_any.at[0, :, pl.ds(h * HD, HD)], sems.at[h])
        for h in range(heads)
    ]
    for copy in copies:
        copy.start()
    k_gain = gains_ref[1:2, :]
    for g in range(heads // 4):
        for core in range(2):
            first, second = 4 * g + core, 4 * g + 2 + core
            rows = pl.ds(core * HALF, HALF)
            cols = pl.ds(g * HD, HD)
            both = in_ref[first, BLK : 2 * BLK, :].astype(F32) + in_ref[second, BLK : 2 * BLK, :].astype(F32)
            v_grad_ref[0, rows, cols] = both[HALF:BLK].astype(BF16)
            values = k_ref[0, rows, cols].astype(F32)
            inverse = inverse_rms(values)
            scaled = k_gain * both[0:HALF].astype(BF16).astype(F32)
            total = jnp.sum(scaled * values, axis=-1, keepdims=True)
            grad = inverse * scaled - inverse * inverse * inverse * values * total / HD
            k_grad_ref[0, rows, cols] = grad.astype(BF16)
    for copy in copies:
        copy.wait()


def dp_step(values, step, dp_count):
    if step >= dp_count:
        return values
    return values + lax.ppermute(values, "dp", [(z, z ^ step) for z in range(dp_count)])


def struct(shape, dtype):
    return jax.ShapeDtypeStruct(shape, dtype)


def call(kernel, ins, outs, scratch=(), mib=12, aliases={}):
    return pl.pallas_call(
        kernel,
        out_shape=tuple(array for array, spec in outs),
        in_specs=list(ins),
        out_specs=tuple(spec for array, spec in outs),
        scratch_shapes=list(scratch),
        input_output_aliases=aliases,
        compiler_params=pltpu.CompilerParams(vmem_limit_bytes=mib << 20),
    )


def shards(heads, dp_count, q_raw, k_raw, v_raw, q_gain, k_gain, key_blocks, d_context):
    blocks = heads
    swap = [(s, s ^ 1) for s in range(heads)]
    mine = lax.broadcasted_iota(jnp.int32, (2, HD), 1) // (HD // dp_count) == lax.axis_index("dp")
    spread = jnp.concatenate([jnp.tile(q_gain, dp_count)[None], jnp.tile(k_gain, dp_count)[None]], axis=0)
    gains = jnp.where(mine, spread, 0.0)

    (sent,) = call(
        functools.partial(pack_kernel, heads),
        [HBM_SPEC] * 4,
        [(pltpu.HBM((heads, 3 * BLK, HD), BF16), HBM_SPEC)],
        [
            pltpu.VMEM(q_raw.shape[1:], BF16),
            pltpu.VMEM(d_context.shape[1:], BF16),
            pltpu.VMEM(k_raw.shape[1:], BF16),
            pltpu.VMEM(v_raw.shape[1:], BF16),
            pltpu.VMEM((heads, 3 * BLK, HD), BF16),
            pltpu.SemaphoreType.DMA((4 * PACKS,)),
            pltpu.SemaphoreType.DMA((PACKS,)),
        ],
    )(*[pltpu.with_memory_space_constraint(x, pltpu.HBM) for x in (q_raw, d_context, k_raw, v_raw)])
    arrived = lax.all_to_all(sent, "seq", 0, 0, tiled=True)
    for step in (8, 4, 2, 1):
        gains = dp_step(gains, step, dp_count)
    arrived, gains = lax.optimization_barrier((arrived, gains))
    other = lax.ppermute(arrived[:, 2 * BLK :], "seq", swap)

    send, keep, give, parts = call(
        functools.partial(attend_kernel, blocks),
        [SMEM_SPEC] + [VMEM_SPEC] * 3,
        [
            (pltpu.HBM((blocks, 2 * BLK, HD), BF16), HBM_SPEC),
            (pltpu.HBM((blocks, BLK, HD), BF16), HBM_SPEC),
            (pltpu.HBM((blocks, BLK, HD), BF16), HBM_SPEC),
            (struct((blocks, PARTS, HD), F32), VMEM_SPEC),
        ],
        [
            pltpu.VMEM((blocks, BLK, HD), BF16),
            pltpu.VMEM((blocks, BLK, HD), BF16),
            pltpu.VMEM((blocks, BLK, HD), BF16),
            pltpu.VMEM((blocks, BLK, 2 * HD), F32),
            pltpu.VMEM((blocks * BLK, 2 * BLK), F32),
            pltpu.VMEM((HD, BLK), F32),
            pltpu.VMEM((blocks, BLK, 2 * HD), BF16),
            pltpu.VMEM((blocks, HD, BLK), BF16),
            pltpu.VMEM((blocks, BLK, HD), F32),
            pltpu.VMEM((blocks, BLK, HD), BF16),
        ]
        + [pltpu.VMEM((SLOTS * BLK, BLK), F32)] * 4
        + [pltpu.VMEM((SLOTS * BLK, BLK), BF16)] * 2
        + [pltpu.VMEM((2, 8, BLK), F32), pltpu.SemaphoreType.DMA]
        + [pltpu.SemaphoreType.DMA((OUTS,))] * 2,
        mib=40,
    )(key_blocks, gains, arrived, other)

    parts = lax.all_to_all(parts, "seq", 0, 0, tiled=True)
    got = lax.ppermute(give, "seq", swap)
    (send,) = call(
        functools.partial(merge_kernel, blocks),
        [VMEM_SPEC] * 2 + [HBM_SPEC],
        [(pltpu.HBM(send.shape, BF16), HBM_SPEC)],
        [pltpu.VMEM((blocks, BLK, HD), BF16), pltpu.SemaphoreType.DMA],
        aliases={2: 0},
    )(keep, got, send)
    back = lax.all_to_all(send, "seq", 0, 0, tiled=True)

    (totals,) = call(parts_sum_kernel, [VMEM_SPEC], [(struct((2, HD), F32), VMEM_SPEC)])(parts)
    for step in (8, 4, 2):
        totals = dp_step(totals, step, dp_count)
    totals = dp_step(totals, 1, dp_count)
    width = q_gain.shape[0]
    totals = lax.dynamic_slice_in_dim(totals, lax.axis_index("dp") * width, width, axis=1)

    q_grad, k_grad, v_grad = call(
        functools.partial(final_kernel, heads),
        [VMEM_SPEC] * 3,
        [
            (struct(q_raw.shape, BF16), HBM_SPEC),
            (struct(k_raw.shape, BF16), VMEM_SPEC),
            (struct(v_raw.shape, BF16), VMEM_SPEC),
        ],
        [pltpu.SemaphoreType.DMA((heads,))],
    )(back, k_raw, gains)
    return (q_grad, k_grad, v_grad, totals[0], totals[1])


def solution(mesh):
    placed = (
        P("dp", "seq", None),
        P("dp", "seq", None),
        P("dp", "seq", None),
        P("dp"),
        P("dp"),
        P("seq", None, None),
        P("dp", "seq", None),
    )
    return jax.shard_map(
        functools.partial(shards, mesh.shape["seq"], mesh.shape["dp"]),
        mesh=mesh,
        in_specs=placed,
        out_specs=(
            P("dp", "seq", None),
            P("dp", "seq", None),
            P("dp", "seq", None),
            P("dp"),
            P("dp"),
        ),
        check_vma=False,
    )
```

```python
import functools
import math

import jax
import jax.numpy as jnp
from jax import lax
from jax.experimental import pallas as pl
from jax.experimental.pallas import tpu as pltpu
from jax.sharding import PartitionSpec as P

BLK = 128
HD = 128
HALF = BLK // 2
SLOTS = 6
PARTS = 8
PACKS = 4
OUTS = 4
EPSILON = 1e-06

F32 = jnp.float32
BF16 = jnp.bfloat16
NT = (((1,), (1,)), ((), ()))
NN = (((1,), (0,)), ((), ()))

VMEM_SPEC = pl.BlockSpec(memory_space=pltpu.VMEM)
SMEM_SPEC = pl.BlockSpec(memory_space=pltpu.SMEM)
HBM_SPEC = pl.BlockSpec(memory_space=pltpu.HBM)


def pack_kernel(heads, q_any, d_any, k_any, v_any, out_any, q_ref, d_ref, k_ref, v_ref, out_ref, sems, out_sems):
    step = heads // PACKS
    loads = []
    for n in range(PACKS):
        wide = pl.ds(n * step * HD, step * HD)
        cols = pl.ds(n * (step // 4) * HD, (step // 4) * HD)
        arrays = ((q_any, q_ref, wide), (d_any, d_ref, wide), (k_any, k_ref, cols), (v_any, v_ref, cols))
        loads.append(
            [
                pltpu.make_async_copy(source.at[0, :, span], held.at[:, span], sems.at[4 * n + i])
                for i, (source, held, span) in enumerate(arrays)
            ]
        )
    for group in loads:
        for copy in group:
            copy.start()
    outs = []
    for n in range(PACKS):
        for copy in loads[n]:
            copy.wait()
        for h in range(n * step, (n + 1) * step):
            half = (h % 2) * HALF
            rows = slice(half, half + HALF)
            wide = slice(h * HD, (h + 1) * HD)
            cols = slice((h // 4) * HD, (h // 4 + 1) * HD)
            out_ref[h, 0:BLK, :] = q_ref[:, wide]
            out_ref[h, BLK : 2 * BLK, :] = d_ref[:, wide]
            out_ref[h, 2 * BLK : 2 * BLK + HALF, :] = k_ref[rows, cols]
            out_ref[h, 2 * BLK + HALF : 3 * BLK, :] = v_ref[rows, cols]
        chunk = pl.ds(n * step, step)
        outs.append(pltpu.make_async_copy(out_ref.at[chunk], out_any.at[chunk], out_sems.at[n]))
        outs[-1].start()
    for copy in outs:
        copy.wait()


def inverse_rms(values):
    return lax.rsqrt(jnp.mean(values * values, axis=-1, keepdims=True) + EPSILON)


def rows_sum(values):
    return jnp.sum(values.reshape(values.shape[0] // 8, 8, values.shape[1]), axis=0)


def named_blocks(pat_ref, b):
    named = [pat_ref[0, b, s] for s in range(SLOTS)]
    return named, [jnp.maximum(n, 0) for n in named]


SCALE = 1.0 / math.sqrt(HD)
SCALE2 = SCALE * math.log2(math.e)
CHUNK = 8
GROUPS = [list(range(s, s + 2)) for s in range(0, SLOTS, 2)]


def attend_kernel(
    blocks, pat_ref, gains_ref, got_ref, other_ref,
    send_any, keep_any, give_any, parts_ref,
    dq_ref, keep_ref, give_ref, acc_ref, lead_ref, lead_dq_ref, kv_ref, kt_ref, khat_ref, qn_ref,
    s0, s1, g0, g1, x0, x1, peak_ref, sem, give_sems, keep_sems,
):
    s_refs, g_refs, x_refs = (s0, s1), (g0, g1), (x0, x1)
    q_gain = gains_ref[0:1, :]
    k_gain = gains_ref[1:2, :]
    zeros = jnp.zeros((BLK, HD), BF16)
    own_k, own_v = pl.ds(2 * BLK, HALF), pl.ds(2 * BLK + HALF, HALF)

    def normalise(j, carry):
        k_raw = jnp.concatenate([got_ref[j, own_k, :], other_ref[j, 0:HALF, :]], axis=0).astype(F32)
        k_hat = k_raw * inverse_rms(k_raw)
        k_low = (k_hat * k_gain).astype(BF16)
        q_raw = got_ref[j, 0:BLK, :].astype(F32)
        q_low = (q_raw * inverse_rms(q_raw) * q_gain).astype(BF16)
        khat_ref[j] = k_hat
        kv_ref[j, :, 0:HD] = k_low
        kv_ref[j, :, HD : 2 * HD] = jnp.concatenate([got_ref[j, own_v, :], other_ref[j, HALF:BLK, :]], axis=0)
        kt_ref[j] = k_low.T
        qn_ref[j] = q_low
        return carry

    lax.fori_loop(0, blocks, normalise, 0, unroll=4)

    def pair_of(b):
        d_low = got_ref[b, BLK : 2 * BLK, :]
        return jnp.concatenate(
            [jnp.concatenate([qn_ref[b], zeros], axis=1), jnp.concatenate([zeros, d_low], axis=1)], axis=0
        )

    def slot_rows(s):
        return pl.ds(s * BLK, BLK)

    pair = pair_of(0)

    def chunk_rows(i):
        return pl.ds(pl.multiple_of(i * CHUNK * BLK, CHUNK * BLK), CHUNK * BLK)

    def lead_scores(i, peak):
        rows = kv_ref[pl.ds(i * CHUNK, CHUNK)].reshape(CHUNK * BLK, 2 * HD)
        both = lax.dot_general(rows, pair, NT, preferred_element_type=F32)
        lead_ref[chunk_rows(i), :] = both
        return jnp.maximum(peak, jnp.max(both[:, 0:BLK].reshape(CHUNK * BLK // 8, 8, BLK), axis=0))

    peak = lax.fori_loop(0, blocks // CHUNK, lead_scores, jnp.full((8, BLK), -jnp.inf, F32))
    peak = jnp.max(peak, axis=0, keepdims=True) * SCALE2

    def lead_exp(i, sums):
        raised = jnp.exp2(lead_ref[chunk_rows(i), 0:BLK] * SCALE2 - peak)
        lead_ref[chunk_rows(i), 0:BLK] = raised
        product = raised * lead_ref[chunk_rows(i), BLK : 2 * BLK]
        return sums[0] + rows_sum(raised), sums[1] + rows_sum(product)

    zero8 = jnp.zeros((8, BLK), F32)
    total, delta = lax.fori_loop(0, blocks // CHUNK, lead_exp, (zero8, zero8))
    lead_inv = 1.0 / jnp.sum(total, axis=0, keepdims=True)
    lead_delta = jnp.sum(delta, axis=0, keepdims=True) * lead_inv

    def lead_grad(i, dq_t):
        weights = lead_ref[chunk_rows(i), 0:BLK] * lead_inv
        d_weights = lead_ref[chunk_rows(i), BLK : 2 * BLK]
        d_low = (weights * (d_weights - lead_delta) * SCALE).astype(BF16)
        both = jnp.concatenate([d_low, weights.astype(BF16)], axis=1)
        terms = lax.dot_general(both, pair, NN, preferred_element_type=F32)
        acc_ref[pl.ds(i * CHUNK, CHUNK)] = terms.reshape(CHUNK, BLK, 2 * HD)
        keys = jnp.concatenate([kt_ref[i * CHUNK + t] for t in range(CHUNK)], axis=1)
        return dq_t + lax.dot_general(keys, d_low, NN, preferred_element_type=F32)

    lead_dq_ref[...] = lax.fori_loop(0, blocks // CHUNK, lead_grad, jnp.zeros((HD, BLK), F32))

    def scores_slots(b, side, slots, pair, peak):
        index = named_blocks(pat_ref, b)[1]
        rows = jnp.concatenate([kv_ref[index[s]] for s in slots], axis=0)
        both = lax.dot_general(rows, pair, NT, preferred_element_type=F32)
        span = pl.ds(slots[0] * BLK, len(slots) * BLK)
        s_refs[side][span, :] = both[:, 0:BLK]
        g_refs[side][span, :] = both[:, BLK : 2 * BLK]
        top = jnp.max(both[:, 0:BLK].reshape(len(slots) * BLK // 8, 8, BLK), axis=0)
        return top if peak is None else jnp.maximum(peak, top)

    def exp_slot(b, side, s, peak, sums):
        named = named_blocks(pat_ref, b)[0]
        kept = named[s] >= 0
        for t in range(s):
            kept = jnp.logical_and(kept, named[s] != named[t])
        floor = peak + jnp.where(kept, 0.0, jnp.inf).astype(F32)
        raised = jnp.exp2(s_refs[side][slot_rows(s), :] * SCALE2 - floor)
        s_refs[side][slot_rows(s), :] = raised
        product = raised * g_refs[side][slot_rows(s), :]
        return sums[0] + rows_sum(raised), sums[1] + rows_sum(product)

    def grads_slots(side, slots, pair, inv_total, inv_scaled, delta):
        span = pl.ds(slots[0] * BLK, len(slots) * BLK)
        raised = s_refs[side][span, :]
        d_low = (raised * inv_scaled * (g_refs[side][span, :] - delta)).astype(BF16)
        x_refs[side][span, :] = d_low
        both = jnp.concatenate([d_low, (raised * inv_total).astype(BF16)], axis=1)
        return lax.dot_general(both, pair, NN, preferred_element_type=F32)

    def query_product(b, side):
        index = named_blocks(pat_ref, b)[1]
        keys = jnp.concatenate([kt_ref[i] for i in index], axis=1)
        return lax.dot_general(keys, x_refs[side][...], NN, preferred_element_type=F32)

    def query_grad(b, dq_t, q_part):
        dq = dq_t.T.astype(BF16).astype(F32)
        q_raw = got_ref[b, 0:BLK, :].astype(F32)
        q_inv = inverse_rms(q_raw)
        q_hat = q_raw * q_inv
        scaled = q_gain * dq
        mean = jnp.mean(scaled * q_hat, axis=-1, keepdims=True)
        dq_ref[b] = (q_inv * (scaled - q_hat * mean)).astype(BF16)
        return q_part + rows_sum(dq * q_hat)

    def step(b, side, q_part, ahead=True, behind=True):
        peak = peak_ref[side, 0:1, :] * SCALE2
        sums = (zero8, zero8)
        pair = pair_of(b + 1) if ahead else None
        top = None
        dq_t = query_product(b - 1, 1 - side) if behind else None
        for slots in GROUPS:
            if ahead:
                top = scores_slots(b + 1, 1 - side, slots, pair, top)
            for s in slots:
                sums = exp_slot(b, side, s, peak, sums)
        if ahead:
            peak_ref[1 - side, 0:1, :] = jnp.max(top, axis=0, keepdims=True)
        inv_total = 1.0 / jnp.sum(sums[0], axis=0, keepdims=True)
        delta = jnp.sum(sums[1], axis=0, keepdims=True) * inv_total
        pair = pair_of(b)
        index = named_blocks(pat_ref, b)[1]
        for slots in GROUPS:
            terms = grads_slots(side, slots, pair, inv_total, inv_total * SCALE, delta)
            for n, s in enumerate(slots):
                acc_ref[index[s]] += terms[n * BLK : (n + 1) * BLK]
        return query_grad(b - 1, dq_t, q_part) if behind else q_part

    x0[...] = jnp.zeros_like(x0)
    pair = pair_of(1)
    top = None
    for slots in GROUPS:
        top = scores_slots(1, 1, slots, pair, top)
    peak_ref[1, 0:1, :] = jnp.max(top, axis=0, keepdims=True)

    def two_steps(i, q_part):
        q_part = step(2 * i + 1, 1, q_part)
        return step(2 * i + 2, 0, q_part)

    q_part = lax.fori_loop(0, blocks // 2 - 1, two_steps, zero8)
    q_part = step(blocks - 1, 1, q_part, ahead=False)
    q_part = query_grad(blocks - 1, query_product(blocks - 1, 1), q_part)
    q_part = query_grad(0, lead_dq_ref[...], q_part)
    dq_copy = pltpu.make_async_copy(dq_ref, send_any.at[:, pl.ds(0, BLK)], sem)
    dq_copy.start()

    def finish(j, k_part):
        for half, ref in ((0, keep_ref), (HALF, give_ref)):
            rows = pl.ds(half, HALF)
            ref[j, 0:HALF, :] = acc_ref[j, rows, 0:HD].astype(BF16)
            ref[j, HALF:BLK, :] = acc_ref[j, rows, HD : 2 * HD].astype(BF16)
        return k_part + rows_sum(acc_ref[j, :, 0:HD] * khat_ref[j])

    k_part = zero8
    step_blocks = blocks // OUTS
    out_copies = []
    for n in range(OUTS):
        k_part = lax.fori_loop(n * step_blocks, (n + 1) * step_blocks, finish, k_part, unroll=2)
        chunk = pl.ds(n * step_blocks, step_blocks)
        for ref, out, copy_sems in ((give_ref, give_any, give_sems), (keep_ref, keep_any, keep_sems)):
            out_copies.append(pltpu.make_async_copy(ref.at[chunk], out.at[chunk], copy_sems.at[n]))
            out_copies[-1].start()
    parts = jnp.concatenate(
        [
            jnp.sum(q_part, axis=0, keepdims=True),
            jnp.sum(k_part, axis=0, keepdims=True),
            jnp.zeros((PARTS - 2, HD), F32),
        ],
        axis=0,
    )
    for j in range(blocks):
        parts_ref[j] = parts
    dq_copy.wait()
    for copy in out_copies:
        copy.wait()


def merge_kernel(blocks, keep_any, got_ref, send_any, out_any, keep_ref, sum_ref, sems, out_sems):
    step = blocks // OUTS
    loads = []
    for n in range(OUTS):
        chunk = pl.ds(n * step, step)
        loads.append(pltpu.make_async_copy(keep_any.at[chunk], keep_ref.at[chunk], sems.at[n]))
        loads[-1].start()

    def one_block(j, carry):
        sum_ref[j] = (keep_ref[j].astype(F32) + got_ref[j].astype(F32)).astype(BF16)
        return carry

    outs = []
    for n in range(OUTS):
        loads[n].wait()
        lax.fori_loop(n * step, (n + 1) * step, one_block, 0, unroll=4)
        chunk = pl.ds(n * step, step)
        outs.append(
            pltpu.make_async_copy(sum_ref.at[chunk], out_any.at[chunk, pl.ds(BLK, BLK)], out_sems.at[n])
        )
        outs[-1].start()
    for copy in outs:
        copy.wait()


def parts_sum_kernel(in_ref, out_ref):
    out_ref[...] = jnp.sum(in_ref[...], axis=0)[0:2]


def final_kernel(heads, in_ref, k_ref, gains_ref, q_grad_any, k_grad_ref, v_grad_ref, sems):
    copies = [
        pltpu.make_async_copy(in_ref.at[h, pl.ds(0, BLK)], q_grad_any.at[0, :, pl.ds(h * HD, HD)], sems.at[h])
        for h in range(heads)
    ]
    for copy in copies:
        copy.start()
    k_gain = gains_ref[1:2, :]
    for g in range(heads // 4):
        for core in range(2):
            first, second = 4 * g + core, 4 * g + 2 + core
            rows = pl.ds(core * HALF, HALF)
            cols = pl.ds(g * HD, HD)
            both = in_ref[first, BLK : 2 * BLK, :].astype(F32) + in_ref[second, BLK : 2 * BLK, :].astype(F32)
            v_grad_ref[0, rows, cols] = both[HALF:BLK].astype(BF16)
            values = k_ref[0, rows, cols].astype(F32)
            inverse = inverse_rms(values)
            scaled = k_gain * both[0:HALF].astype(BF16).astype(F32)
            total = jnp.sum(scaled * values, axis=-1, keepdims=True)
            grad = inverse * scaled - inverse * inverse * inverse * values * total / HD
            k_grad_ref[0, rows, cols] = grad.astype(BF16)
    for copy in copies:
        copy.wait()


def dp_step(values, step, dp_count):
    if step >= dp_count:
        return values
    return values + lax.ppermute(values, "dp", [(z, z ^ step) for z in range(dp_count)])


def struct(shape, dtype):
    return jax.ShapeDtypeStruct(shape, dtype)


def call(kernel, ins, outs, scratch=(), mib=12, aliases={}):
    return pl.pallas_call(
        kernel,
        out_shape=tuple(array for array, spec in outs),
        in_specs=list(ins),
        out_specs=tuple(spec for array, spec in outs),
        scratch_shapes=list(scratch),
        input_output_aliases=aliases,
        compiler_params=pltpu.CompilerParams(vmem_limit_bytes=mib << 20),
    )


def shards(heads, dp_count, q_raw, k_raw, v_raw, q_gain, k_gain, key_blocks, d_context):
    blocks = heads
    swap = [(s, s ^ 1) for s in range(heads)]
    mine = lax.broadcasted_iota(jnp.int32, (2, HD), 1) // (HD // dp_count) == lax.axis_index("dp")
    spread = jnp.concatenate([jnp.tile(q_gain, dp_count)[None], jnp.tile(k_gain, dp_count)[None]], axis=0)
    gains = jnp.where(mine, spread, 0.0)

    (sent,) = call(
        functools.partial(pack_kernel, heads),
        [HBM_SPEC] * 4,
        [(pltpu.HBM((heads, 3 * BLK, HD), BF16), HBM_SPEC)],
        [
            pltpu.VMEM(q_raw.shape[1:], BF16),
            pltpu.VMEM(d_context.shape[1:], BF16),
            pltpu.VMEM(k_raw.shape[1:], BF16),
            pltpu.VMEM(v_raw.shape[1:], BF16),
            pltpu.VMEM((heads, 3 * BLK, HD), BF16),
            pltpu.SemaphoreType.DMA((4 * PACKS,)),
            pltpu.SemaphoreType.DMA((PACKS,)),
        ],
    )(*[pltpu.with_memory_space_constraint(x, pltpu.HBM) for x in (q_raw, d_context, k_raw, v_raw)])
    arrived = lax.all_to_all(sent, "seq", 0, 0, tiled=True)
    for step in (8, 4, 2, 1):
        gains = dp_step(gains, step, dp_count)
    arrived, gains = lax.optimization_barrier((arrived, gains))
    other = lax.ppermute(arrived[:, 2 * BLK :], "seq", swap)

    send, keep, give, parts = call(
        functools.partial(attend_kernel, blocks),
        [SMEM_SPEC] + [VMEM_SPEC] * 3,
        [
            (pltpu.HBM((blocks, 2 * BLK, HD), BF16), HBM_SPEC),
            (pltpu.HBM((blocks, BLK, HD), BF16), HBM_SPEC),
            (pltpu.HBM((blocks, BLK, HD), BF16), HBM_SPEC),
            (struct((blocks, PARTS, HD), F32), VMEM_SPEC),
        ],
        [
            pltpu.VMEM((blocks, BLK, HD), BF16),
            pltpu.VMEM((blocks, BLK, HD), BF16),
            pltpu.VMEM((blocks, BLK, HD), BF16),
            pltpu.VMEM((blocks, BLK, 2 * HD), F32),
            pltpu.VMEM((blocks * BLK, 2 * BLK), F32),
            pltpu.VMEM((HD, BLK), F32),
            pltpu.VMEM((blocks, BLK, 2 * HD), BF16),
            pltpu.VMEM((blocks, HD, BLK), BF16),
            pltpu.VMEM((blocks, BLK, HD), F32),
            pltpu.VMEM((blocks, BLK, HD), BF16),
        ]
        + [pltpu.VMEM((SLOTS * BLK, BLK), F32)] * 4
        + [pltpu.VMEM((SLOTS * BLK, BLK), BF16)] * 2
        + [pltpu.VMEM((2, 8, BLK), F32), pltpu.SemaphoreType.DMA]
        + [pltpu.SemaphoreType.DMA((OUTS,))] * 2,
        mib=40,
    )(key_blocks, gains, arrived, other)

    parts = lax.all_to_all(parts, "seq", 0, 0, tiled=True)
    got = lax.ppermute(give, "seq", swap)
    (send,) = call(
        functools.partial(merge_kernel, blocks),
        [HBM_SPEC, VMEM_SPEC, HBM_SPEC],
        [(pltpu.HBM(send.shape, BF16), HBM_SPEC)],
        [pltpu.VMEM((blocks, BLK, HD), BF16)] * 2 + [pltpu.SemaphoreType.DMA((OUTS,))] * 2,
        aliases={2: 0},
    )(pltpu.with_memory_space_constraint(keep, pltpu.HBM), got, send)
    back = lax.all_to_all(send, "seq", 0, 0, tiled=True)

    (totals,) = call(parts_sum_kernel, [VMEM_SPEC], [(struct((2, HD), F32), VMEM_SPEC)])(parts)
    totals = dp_step(totals, 1, dp_count)
    for step in (8, 4):
        totals = dp_step(totals, step, dp_count)
    totals = dp_step(totals, 2, dp_count)
    width = q_gain.shape[0]
    totals = lax.dynamic_slice_in_dim(totals, lax.axis_index("dp") * width, width, axis=1)

    q_grad, k_grad, v_grad = call(
        functools.partial(final_kernel, heads),
        [VMEM_SPEC] * 3,
        [
            (struct(q_raw.shape, BF16), HBM_SPEC),
            (struct(k_raw.shape, BF16), VMEM_SPEC),
            (struct(v_raw.shape, BF16), VMEM_SPEC),
        ],
        [pltpu.SemaphoreType.DMA((heads,))],
    )(back, k_raw, gains)
    return (q_grad, k_grad, v_grad, totals[0], totals[1])


def solution(mesh):
    placed = (
        P("dp", "seq", None),
        P("dp", "seq", None),
        P("dp", "seq", None),
        P("dp"),
        P("dp"),
        P("seq", None, None),
        P("dp", "seq", None),
    )
    return jax.shard_map(
        functools.partial(shards, mesh.shape["seq"], mesh.shape["dp"]),
        mesh=mesh,
        in_specs=placed,
        out_specs=(
            P("dp", "seq", None),
            P("dp", "seq", None),
            P("dp", "seq", None),
            P("dp"),
            P("dp"),
        ),
        check_vma=False,
    )
```

```python
import functools
import math

import jax
import jax.numpy as jnp
from jax import lax
from jax.experimental import pallas as pl
from jax.experimental.pallas import tpu as pltpu
from jax.sharding import PartitionSpec as P

BLK = 128
HD = 128
HALF = BLK // 2
SLOTS = 6
PARTS = 8
PACKS = 4
OUTS = 4
EPSILON = 1e-06

F32 = jnp.float32
BF16 = jnp.bfloat16
NT = (((1,), (1,)), ((), ()))
NN = (((1,), (0,)), ((), ()))

VMEM_SPEC = pl.BlockSpec(memory_space=pltpu.VMEM)
SMEM_SPEC = pl.BlockSpec(memory_space=pltpu.SMEM)
HBM_SPEC = pl.BlockSpec(memory_space=pltpu.HBM)


def pack_kernel(heads, q_any, d_any, k_any, v_any, out_any, q_ref, d_ref, k_ref, v_ref, out_ref, sems, out_sems):
    step = heads // PACKS
    loads = []
    for n in range(PACKS):
        wide = pl.ds(n * step * HD, step * HD)
        cols = pl.ds(n * (step // 4) * HD, (step // 4) * HD)
        arrays = ((q_any, q_ref, wide), (d_any, d_ref, wide), (k_any, k_ref, cols), (v_any, v_ref, cols))
        loads.append(
            [
                pltpu.make_async_copy(source.at[0, :, span], held.at[:, span], sems.at[4 * n + i])
                for i, (source, held, span) in enumerate(arrays)
            ]
        )
    for group in loads:
        for copy in group:
            copy.start()
    outs = []
    for n in range(PACKS):
        for copy in loads[n]:
            copy.wait()
        for h in range(n * step, (n + 1) * step):
            half = (h % 2) * HALF
            rows = slice(half, half + HALF)
            wide = slice(h * HD, (h + 1) * HD)
            cols = slice((h // 4) * HD, (h // 4 + 1) * HD)
            out_ref[h, 0:BLK, :] = q_ref[:, wide]
            out_ref[h, BLK : 2 * BLK, :] = d_ref[:, wide]
            out_ref[h, 2 * BLK : 2 * BLK + HALF, :] = k_ref[rows, cols]
            out_ref[h, 2 * BLK + HALF : 3 * BLK, :] = v_ref[rows, cols]
        chunk = pl.ds(n * step, step)
        outs.append(pltpu.make_async_copy(out_ref.at[chunk], out_any.at[chunk], out_sems.at[n]))
        outs[-1].start()
    for copy in outs:
        copy.wait()


def inverse_rms(values):
    return lax.rsqrt(jnp.mean(values * values, axis=-1, keepdims=True) + EPSILON)


def rows_sum(values):
    return jnp.sum(values.reshape(values.shape[0] // 8, 8, values.shape[1]), axis=0)


def named_blocks(pat_ref, b):
    named = [pat_ref[0, b, s] for s in range(SLOTS)]
    return named, [jnp.maximum(n, 0) for n in named]


SCALE = 1.0 / math.sqrt(HD)
SCALE2 = SCALE * math.log2(math.e)
CHUNK = 16
GROUPS = [list(range(s, s + 2)) for s in range(0, SLOTS, 2)]


def attend_kernel(
    blocks, pat_ref, gains_ref, got_ref, other_any,
    send_any, keep_any, give_any, parts_ref,
    other_ref, dq_ref, keep_ref, give_ref, acc_ref, lead_ref, lead_dq_ref, kv_ref, kt_ref, khat_ref, qn_ref,
    s0, s1, g0, g1, x0, x1, peak_ref, sem, other_sem, give_sems, keep_sems,
):
    s_refs, g_refs, x_refs = (s0, s1), (g0, g1), (x0, x1)
    q_gain = gains_ref[0:1, :]
    k_gain = gains_ref[1:2, :]
    zeros = jnp.zeros((BLK, HD), BF16)
    own_k, own_v = pl.ds(2 * BLK, HALF), pl.ds(2 * BLK + HALF, HALF)

    def normalise_queries(j, carry):
        q_raw = got_ref[j, 0:BLK, :].astype(F32)
        qn_ref[j] = (q_raw * inverse_rms(q_raw) * q_gain).astype(BF16)
        return carry

    def normalise_keys(j, carry):
        k_raw = jnp.concatenate([got_ref[j, own_k, :], other_ref[j, 0:HALF, :]], axis=0).astype(F32)
        k_hat = k_raw * inverse_rms(k_raw)
        k_low = (k_hat * k_gain).astype(BF16)
        khat_ref[j] = k_hat
        kv_ref[j, :, 0:HD] = k_low
        kv_ref[j, :, HD : 2 * HD] = jnp.concatenate([got_ref[j, own_v, :], other_ref[j, HALF:BLK, :]], axis=0)
        kt_ref[j] = k_low.T
        return carry

    other_copy = pltpu.make_async_copy(other_any, other_ref, other_sem)
    other_copy.start()
    lax.fori_loop(0, blocks, normalise_queries, 0, unroll=8)
    other_copy.wait()
    lax.fori_loop(0, blocks, normalise_keys, 0, unroll=4)

    def pair_of(b):
        d_low = got_ref[b, BLK : 2 * BLK, :]
        return jnp.concatenate(
            [jnp.concatenate([qn_ref[b], zeros], axis=1), jnp.concatenate([zeros, d_low], axis=1)], axis=0
        )

    def slot_rows(s):
        return pl.ds(s * BLK, BLK)

    pair = pair_of(0)

    def chunk_rows(i):
        return pl.ds(pl.multiple_of(i * CHUNK * BLK, CHUNK * BLK), CHUNK * BLK)

    def lead_scores(i, peak):
        rows = kv_ref[pl.ds(i * CHUNK, CHUNK)].reshape(CHUNK * BLK, 2 * HD)
        both = lax.dot_general(rows, pair, NT, preferred_element_type=F32)
        lead_ref[chunk_rows(i), :] = both
        return jnp.maximum(peak, jnp.max(both[:, 0:BLK].reshape(CHUNK * BLK // 8, 8, BLK), axis=0))

    peak = lax.fori_loop(0, blocks // CHUNK, lead_scores, jnp.full((8, BLK), -jnp.inf, F32))
    peak = jnp.max(peak, axis=0, keepdims=True) * SCALE2

    def lead_exp(i, sums):
        raised = jnp.exp2(lead_ref[chunk_rows(i), 0:BLK] * SCALE2 - peak)
        lead_ref[chunk_rows(i), 0:BLK] = raised
        product = raised * lead_ref[chunk_rows(i), BLK : 2 * BLK]
        return sums[0] + rows_sum(raised), sums[1] + rows_sum(product)

    zero8 = jnp.zeros((8, BLK), F32)
    total, delta = lax.fori_loop(0, blocks // CHUNK, lead_exp, (zero8, zero8))
    lead_inv = 1.0 / jnp.sum(total, axis=0, keepdims=True)
    lead_delta = jnp.sum(delta, axis=0, keepdims=True) * lead_inv

    def lead_grad(i, dq_t):
        weights = lead_ref[chunk_rows(i), 0:BLK] * lead_inv
        d_weights = lead_ref[chunk_rows(i), BLK : 2 * BLK]
        d_low = (weights * (d_weights - lead_delta) * SCALE).astype(BF16)
        both = jnp.concatenate([d_low, weights.astype(BF16)], axis=1)
        terms = lax.dot_general(both, pair, NN, preferred_element_type=F32)
        acc_ref[pl.ds(i * CHUNK, CHUNK)] = terms.reshape(CHUNK, BLK, 2 * HD)
        keys = jnp.concatenate([kt_ref[i * CHUNK + t] for t in range(CHUNK)], axis=1)
        return dq_t + lax.dot_general(keys, d_low, NN, preferred_element_type=F32)

    lead_dq_ref[...] = lax.fori_loop(0, blocks // CHUNK, lead_grad, jnp.zeros((HD, BLK), F32))

    def scores_slots(b, side, slots, pair, peak):
        index = named_blocks(pat_ref, b)[1]
        rows = jnp.concatenate([kv_ref[index[s]] for s in slots], axis=0)
        both = lax.dot_general(rows, pair, NT, preferred_element_type=F32)
        span = pl.ds(slots[0] * BLK, len(slots) * BLK)
        s_refs[side][span, :] = both[:, 0:BLK]
        g_refs[side][span, :] = both[:, BLK : 2 * BLK]
        top = jnp.max(both[:, 0:BLK].reshape(len(slots) * BLK // 8, 8, BLK), axis=0)
        return top if peak is None else jnp.maximum(peak, top)

    def exp_slot(b, side, s, peak, sums):
        named = named_blocks(pat_ref, b)[0]
        kept = named[s] >= 0
        for t in range(s):
            kept = jnp.logical_and(kept, named[s] != named[t])
        floor = peak + jnp.where(kept, 0.0, jnp.inf).astype(F32)
        raised = jnp.exp2(s_refs[side][slot_rows(s), :] * SCALE2 - floor)
        s_refs[side][slot_rows(s), :] = raised
        product = raised * g_refs[side][slot_rows(s), :]
        return sums[0] + rows_sum(raised), sums[1] + rows_sum(product)

    def grads_slots(side, slots, pair, inv_total, inv_scaled, delta):
        span = pl.ds(slots[0] * BLK, len(slots) * BLK)
        raised = s_refs[side][span, :]
        d_low = (raised * inv_scaled * (g_refs[side][span, :] - delta)).astype(BF16)
        x_refs[side][span, :] = d_low
        both = jnp.concatenate([d_low, (raised * inv_total).astype(BF16)], axis=1)
        return lax.dot_general(both, pair, NN, preferred_element_type=F32)

    def query_product(b, side):
        index = named_blocks(pat_ref, b)[1]
        keys = jnp.concatenate([kt_ref[i] for i in index], axis=1)
        return lax.dot_general(keys, x_refs[side][...], NN, preferred_element_type=F32)

    def query_grad(b, dq_t, q_part):
        dq = dq_t.T.astype(BF16).astype(F32)
        q_raw = got_ref[b, 0:BLK, :].astype(F32)
        q_inv = inverse_rms(q_raw)
        q_hat = q_raw * q_inv
        scaled = q_gain * dq
        mean = jnp.mean(scaled * q_hat, axis=-1, keepdims=True)
        dq_ref[b] = (q_inv * (scaled - q_hat * mean)).astype(BF16)
        return q_part + rows_sum(dq * q_hat)

    def step(b, side, q_part, ahead=True, behind=True):
        peak = peak_ref[side, 0:1, :] * SCALE2
        sums = (zero8, zero8)
        pair = pair_of(b + 1) if ahead else None
        top = None
        dq_t = query_product(b - 1, 1 - side) if behind else None
        for slots in GROUPS:
            if ahead:
                top = scores_slots(b + 1, 1 - side, slots, pair, top)
            for s in slots:
                sums = exp_slot(b, side, s, peak, sums)
        if ahead:
            peak_ref[1 - side, 0:1, :] = jnp.max(top, axis=0, keepdims=True)
        inv_total = 1.0 / jnp.sum(sums[0], axis=0, keepdims=True)
        delta = jnp.sum(sums[1], axis=0, keepdims=True) * inv_total
        pair = pair_of(b)
        index = named_blocks(pat_ref, b)[1]
        for slots in GROUPS:
            terms = grads_slots(side, slots, pair, inv_total, inv_total * SCALE, delta)
            for n, s in enumerate(slots):
                acc_ref[index[s]] += terms[n * BLK : (n + 1) * BLK]
        return query_grad(b - 1, dq_t, q_part) if behind else q_part

    x0[...] = jnp.zeros_like(x0)
    pair = pair_of(1)
    top = None
    for slots in GROUPS:
        top = scores_slots(1, 1, slots, pair, top)
    peak_ref[1, 0:1, :] = jnp.max(top, axis=0, keepdims=True)

    def two_steps(i, q_part):
        q_part = step(2 * i + 1, 1, q_part)
        return step(2 * i + 2, 0, q_part)

    q_part = lax.fori_loop(0, blocks // 2 - 1, two_steps, zero8)
    q_part = step(blocks - 1, 1, q_part, ahead=False)
    q_part = query_grad(blocks - 1, query_product(blocks - 1, 1), q_part)
    q_part = query_grad(0, lead_dq_ref[...], q_part)
    dq_copy = pltpu.make_async_copy(dq_ref, send_any.at[:, pl.ds(0, BLK)], sem)
    dq_copy.start()

    def finish(j, k_part):
        for half, ref in ((0, keep_ref), (HALF, give_ref)):
            rows = pl.ds(half, HALF)
            ref[j, 0:HALF, :] = acc_ref[j, rows, 0:HD].astype(BF16)
            ref[j, HALF:BLK, :] = acc_ref[j, rows, HD : 2 * HD].astype(BF16)
        return k_part + rows_sum(acc_ref[j, :, 0:HD] * khat_ref[j])

    k_part = zero8
    step_blocks = blocks // OUTS
    out_copies = []
    for n in range(OUTS):
        k_part = lax.fori_loop(n * step_blocks, (n + 1) * step_blocks, finish, k_part, unroll=2)
        chunk = pl.ds(n * step_blocks, step_blocks)
        for ref, out, copy_sems in ((give_ref, give_any, give_sems), (keep_ref, keep_any, keep_sems)):
            out_copies.append(pltpu.make_async_copy(ref.at[chunk], out.at[chunk], copy_sems.at[n]))
            out_copies[-1].start()
    parts = jnp.concatenate(
        [
            jnp.sum(q_part, axis=0, keepdims=True),
            jnp.sum(k_part, axis=0, keepdims=True),
            jnp.zeros((PARTS - 2, HD), F32),
        ],
        axis=0,
    )
    for j in range(blocks):
        parts_ref[j] = parts
    dq_copy.wait()
    for copy in out_copies:
        copy.wait()


def merge_kernel(blocks, keep_any, got_ref, send_any, out_any, keep_ref, sum_ref, sems, out_sems):
    step = blocks // OUTS
    loads = []
    for n in range(OUTS):
        chunk = pl.ds(n * step, step)
        loads.append(pltpu.make_async_copy(keep_any.at[chunk], keep_ref.at[chunk], sems.at[n]))
        loads[-1].start()

    def one_block(j, carry):
        sum_ref[j] = (keep_ref[j].astype(F32) + got_ref[j].astype(F32)).astype(BF16)
        return carry

    outs = []
    for n in range(OUTS):
        loads[n].wait()
        lax.fori_loop(n * step, (n + 1) * step, one_block, 0, unroll=4)
        chunk = pl.ds(n * step, step)
        outs.append(
            pltpu.make_async_copy(sum_ref.at[chunk], out_any.at[chunk, pl.ds(BLK, BLK)], out_sems.at[n])
        )
        outs[-1].start()
    for copy in outs:
        copy.wait()


def parts_sum_kernel(in_ref, out_ref):
    out_ref[...] = jnp.sum(in_ref[...], axis=0)[0:2]


def final_kernel(heads, in_ref, k_ref, gains_ref, q_grad_any, k_grad_ref, v_grad_ref, sems):
    copies = [
        pltpu.make_async_copy(in_ref.at[h, pl.ds(0, BLK)], q_grad_any.at[0, :, pl.ds(h * HD, HD)], sems.at[h])
        for h in range(heads)
    ]
    for copy in copies:
        copy.start()
    k_gain = gains_ref[1:2, :]
    for g in range(heads // 4):
        for core in range(2):
            first, second = 4 * g + core, 4 * g + 2 + core
            rows = pl.ds(core * HALF, HALF)
            cols = pl.ds(g * HD, HD)
            both = in_ref[first, BLK : 2 * BLK, :].astype(F32) + in_ref[second, BLK : 2 * BLK, :].astype(F32)
            v_grad_ref[0, rows, cols] = both[HALF:BLK].astype(BF16)
            values = k_ref[0, rows, cols].astype(F32)
            inverse = inverse_rms(values)
            scaled = k_gain * both[0:HALF].astype(BF16).astype(F32)
            total = jnp.sum(scaled * values, axis=-1, keepdims=True)
            grad = inverse * scaled - inverse * inverse * inverse * values * total / HD
            k_grad_ref[0, rows, cols] = grad.astype(BF16)
    for copy in copies:
        copy.wait()


def dp_step(values, step, dp_count):
    if step >= dp_count:
        return values
    return values + lax.ppermute(values, "dp", [(z, z ^ step) for z in range(dp_count)])


def struct(shape, dtype):
    return jax.ShapeDtypeStruct(shape, dtype)


def call(kernel, ins, outs, scratch=(), mib=12, aliases={}):
    return pl.pallas_call(
        kernel,
        out_shape=tuple(array for array, spec in outs),
        in_specs=list(ins),
        out_specs=tuple(spec for array, spec in outs),
        scratch_shapes=list(scratch),
        input_output_aliases=aliases,
        compiler_params=pltpu.CompilerParams(vmem_limit_bytes=mib << 20),
    )


def shards(heads, dp_count, q_raw, k_raw, v_raw, q_gain, k_gain, key_blocks, d_context):
    blocks = heads
    swap = [(s, s ^ 1) for s in range(heads)]
    mine = lax.broadcasted_iota(jnp.int32, (2, HD), 1) // (HD // dp_count) == lax.axis_index("dp")
    spread = jnp.concatenate([jnp.tile(q_gain, dp_count)[None], jnp.tile(k_gain, dp_count)[None]], axis=0)
    gains = jnp.where(mine, spread, 0.0)

    (sent,) = call(
        functools.partial(pack_kernel, heads),
        [HBM_SPEC] * 4,
        [(pltpu.HBM((heads, 3 * BLK, HD), BF16), HBM_SPEC)],
        [
            pltpu.VMEM(q_raw.shape[1:], BF16),
            pltpu.VMEM(d_context.shape[1:], BF16),
            pltpu.VMEM(k_raw.shape[1:], BF16),
            pltpu.VMEM(v_raw.shape[1:], BF16),
            pltpu.VMEM((heads, 3 * BLK, HD), BF16),
            pltpu.SemaphoreType.DMA((4 * PACKS,)),
            pltpu.SemaphoreType.DMA((PACKS,)),
        ],
    )(*[pltpu.with_memory_space_constraint(x, pltpu.HBM) for x in (q_raw, d_context, k_raw, v_raw)])
    arrived = lax.all_to_all(sent, "seq", 0, 0, tiled=True)
    for step in (8, 4, 2, 1):
        gains = dp_step(gains, step, dp_count)
    arrived, gains = lax.optimization_barrier((arrived, gains))
    other = lax.ppermute(arrived[:, 2 * BLK :], "seq", swap)

    send, keep, give, parts = call(
        functools.partial(attend_kernel, blocks),
        [SMEM_SPEC] + [VMEM_SPEC] * 2 + [HBM_SPEC],
        [
            (pltpu.HBM((blocks, 2 * BLK, HD), BF16), HBM_SPEC),
            (pltpu.HBM((blocks, BLK, HD), BF16), HBM_SPEC),
            (pltpu.HBM((blocks, BLK, HD), BF16), HBM_SPEC),
            (struct((blocks, PARTS, HD), F32), VMEM_SPEC),
        ],
        [
            pltpu.VMEM((blocks, BLK, HD), BF16),
            pltpu.VMEM((blocks, BLK, HD), BF16),
            pltpu.VMEM((blocks, BLK, HD), BF16),
            pltpu.VMEM((blocks, BLK, HD), BF16),
            pltpu.VMEM((blocks, BLK, 2 * HD), F32),
            pltpu.VMEM((blocks * BLK, 2 * BLK), F32),
            pltpu.VMEM((HD, BLK), F32),
            pltpu.VMEM((blocks, BLK, 2 * HD), BF16),
            pltpu.VMEM((blocks, HD, BLK), BF16),
            pltpu.VMEM((blocks, BLK, HD), F32),
            pltpu.VMEM((blocks, BLK, HD), BF16),
        ]
        + [pltpu.VMEM((SLOTS * BLK, BLK), F32)] * 4
        + [pltpu.VMEM((SLOTS * BLK, BLK), BF16)] * 2
        + [pltpu.VMEM((2, 8, BLK), F32)]
        + [pltpu.SemaphoreType.DMA] * 2
        + [pltpu.SemaphoreType.DMA((OUTS,))] * 2,
        mib=40,
    )(key_blocks, gains, arrived, pltpu.with_memory_space_constraint(other, pltpu.HBM))

    parts = lax.all_to_all(parts, "seq", 0, 0, tiled=True)
    got = lax.ppermute(give, "seq", swap)
    (send,) = call(
        functools.partial(merge_kernel, blocks),
        [HBM_SPEC, VMEM_SPEC, HBM_SPEC],
        [(pltpu.HBM(send.shape, BF16), HBM_SPEC)],
        [pltpu.VMEM((blocks, BLK, HD), BF16)] * 2 + [pltpu.SemaphoreType.DMA((OUTS,))] * 2,
        aliases={2: 0},
    )(pltpu.with_memory_space_constraint(keep, pltpu.HBM), got, send)
    back = lax.all_to_all(send, "seq", 0, 0, tiled=True)

    (totals,) = call(parts_sum_kernel, [VMEM_SPEC], [(struct((2, HD), F32), VMEM_SPEC)])(parts)
    totals = dp_step(totals, 1, dp_count)
    for step in (8, 4):
        totals = dp_step(totals, step, dp_count)
    totals = dp_step(totals, 2, dp_count)
    width = q_gain.shape[0]
    totals = lax.dynamic_slice_in_dim(totals, lax.axis_index("dp") * width, width, axis=1)

    q_grad, k_grad, v_grad = call(
        functools.partial(final_kernel, heads),
        [VMEM_SPEC] * 3,
        [
            (struct(q_raw.shape, BF16), HBM_SPEC),
            (struct(k_raw.shape, BF16), VMEM_SPEC),
            (struct(v_raw.shape, BF16), VMEM_SPEC),
        ],
        [pltpu.SemaphoreType.DMA((heads,))],
    )(back, k_raw, gains)
    return (q_grad, k_grad, v_grad, totals[0], totals[1])


def solution(mesh):
    placed = (
        P("dp", "seq", None),
        P("dp", "seq", None),
        P("dp", "seq", None),
        P("dp"),
        P("dp"),
        P("seq", None, None),
        P("dp", "seq", None),
    )
    return jax.shard_map(
        functools.partial(shards, mesh.shape["seq"], mesh.shape["dp"]),
        mesh=mesh,
        in_specs=placed,
        out_specs=(
            P("dp", "seq", None),
            P("dp", "seq", None),
            P("dp", "seq", None),
            P("dp"),
            P("dp"),
        ),
        check_vma=False,
    )
```

```python
import functools
import math

import jax
import jax.numpy as jnp
from jax import lax
from jax.experimental import pallas as pl
from jax.experimental.pallas import tpu as pltpu
from jax.sharding import PartitionSpec as P

BLK = 128
HD = 128
HALF = BLK // 2
SLOTS = 6
PARTS = 8
PACKS = 4
OUTS = 4
EPSILON = 1e-06

F32 = jnp.float32
BF16 = jnp.bfloat16
NT = (((1,), (1,)), ((), ()))
NN = (((1,), (0,)), ((), ()))

VMEM_SPEC = pl.BlockSpec(memory_space=pltpu.VMEM)
SMEM_SPEC = pl.BlockSpec(memory_space=pltpu.SMEM)
HBM_SPEC = pl.BlockSpec(memory_space=pltpu.HBM)


def pack_kernel(heads, q_any, d_any, k_any, v_any, out_any, q_ref, d_ref, k_ref, v_ref, out_ref, sems, out_sems):
    step = heads // PACKS
    loads = []
    for n in range(PACKS):
        wide = pl.ds(n * step * HD, step * HD)
        cols = pl.ds(n * (step // 4) * HD, (step // 4) * HD)
        arrays = ((q_any, q_ref, wide), (d_any, d_ref, wide), (k_any, k_ref, cols), (v_any, v_ref, cols))
        loads.append(
            [
                pltpu.make_async_copy(source.at[0, :, span], held.at[:, span], sems.at[4 * n + i])
                for i, (source, held, span) in enumerate(arrays)
            ]
        )
    for group in loads:
        for copy in group:
            copy.start()
    outs = []
    for n in range(PACKS):
        for copy in loads[n]:
            copy.wait()
        for h in range(n * step, (n + 1) * step):
            half = (h % 2) * HALF
            rows = slice(half, half + HALF)
            wide = slice(h * HD, (h + 1) * HD)
            cols = slice((h // 4) * HD, (h // 4 + 1) * HD)
            out_ref[h, 0:BLK, :] = q_ref[:, wide]
            out_ref[h, BLK : 2 * BLK, :] = d_ref[:, wide]
            out_ref[h, 2 * BLK : 2 * BLK + HALF, :] = k_ref[rows, cols]
            out_ref[h, 2 * BLK + HALF : 3 * BLK, :] = v_ref[rows, cols]
        chunk = pl.ds(n * step, step)
        outs.append(pltpu.make_async_copy(out_ref.at[chunk], out_any.at[chunk], out_sems.at[n]))
        outs[-1].start()
    for copy in outs:
        copy.wait()


def inverse_rms(values):
    return lax.rsqrt(jnp.mean(values * values, axis=-1, keepdims=True) + EPSILON)


def rows_sum(values):
    return jnp.sum(values.reshape(values.shape[0] // 8, 8, values.shape[1]), axis=0)


def named_blocks(pat_ref, b):
    named = [pat_ref[0, b, s] for s in range(SLOTS)]
    return named, [jnp.maximum(n, 0) for n in named]


SCALE = 1.0 / math.sqrt(HD)
SCALE2 = SCALE * math.log2(math.e)
CHUNK = 16
GROUPS = [list(range(s, s + 3)) for s in range(0, SLOTS, 3)]
KEY_GROUPS = [list(range(s, s + 2)) for s in range(0, SLOTS, 2)]


def attend_kernel(
    blocks, pat_ref, gains_ref, got_ref, other_any,
    send_any, keep_any, give_any, parts_ref,
    other_ref, dq_ref, keep_ref, give_ref, acc_ref, lead_ref, lead_dq_ref, kv_ref, kt_ref, khat_ref, qn_ref,
    s0, s1, g0, g1, x0, x1, peak_ref, sem, other_sem, give_sems, keep_sems,
):
    s_refs, g_refs, x_refs = (s0, s1), (g0, g1), (x0, x1)
    q_gain = gains_ref[0:1, :]
    k_gain = gains_ref[1:2, :]
    zeros = jnp.zeros((BLK, HD), BF16)
    own_k, own_v = pl.ds(2 * BLK, HALF), pl.ds(2 * BLK + HALF, HALF)

    def normalise_queries(j, carry):
        q_raw = got_ref[j, 0:BLK, :].astype(F32)
        qn_ref[j] = (q_raw * inverse_rms(q_raw) * q_gain).astype(BF16)
        return carry

    def normalise_keys(j, carry):
        k_raw = jnp.concatenate([got_ref[j, own_k, :], other_ref[j, 0:HALF, :]], axis=0).astype(F32)
        k_hat = k_raw * inverse_rms(k_raw)
        k_low = (k_hat * k_gain).astype(BF16)
        khat_ref[j] = k_hat
        kv_ref[j, :, 0:HD] = k_low
        kv_ref[j, :, HD : 2 * HD] = jnp.concatenate([got_ref[j, own_v, :], other_ref[j, HALF:BLK, :]], axis=0)
        kt_ref[j] = k_low.T
        return carry

    other_copy = pltpu.make_async_copy(other_any, other_ref, other_sem)
    other_copy.start()
    lax.fori_loop(0, blocks, normalise_queries, 0, unroll=8)
    other_copy.wait()
    lax.fori_loop(0, blocks, normalise_keys, 0, unroll=8)

    def pair_of(b):
        d_low = got_ref[b, BLK : 2 * BLK, :]
        return jnp.concatenate(
            [jnp.concatenate([qn_ref[b], zeros], axis=1), jnp.concatenate([zeros, d_low], axis=1)], axis=0
        )

    def slot_rows(s):
        return pl.ds(s * BLK, BLK)

    pair = pair_of(0)

    def chunk_rows(i):
        return pl.ds(pl.multiple_of(i * CHUNK * BLK, CHUNK * BLK), CHUNK * BLK)

    def lead_scores(i, peak):
        rows = kv_ref[pl.ds(i * CHUNK, CHUNK)].reshape(CHUNK * BLK, 2 * HD)
        both = lax.dot_general(rows, pair, NT, preferred_element_type=F32)
        lead_ref[chunk_rows(i), :] = both
        return jnp.maximum(peak, jnp.max(both[:, 0:BLK].reshape(CHUNK * BLK // 8, 8, BLK), axis=0))

    peak = lax.fori_loop(0, blocks // CHUNK, lead_scores, jnp.full((8, BLK), -jnp.inf, F32))
    peak = jnp.max(peak, axis=0, keepdims=True) * SCALE2

    def lead_exp(i, sums):
        raised = jnp.exp2(lead_ref[chunk_rows(i), 0:BLK] * SCALE2 - peak)
        lead_ref[chunk_rows(i), 0:BLK] = raised
        product = raised * lead_ref[chunk_rows(i), BLK : 2 * BLK]
        return sums[0] + rows_sum(raised), sums[1] + rows_sum(product)

    zero8 = jnp.zeros((8, BLK), F32)
    total, delta = lax.fori_loop(0, blocks // CHUNK, lead_exp, (zero8, zero8))
    lead_inv = 1.0 / jnp.sum(total, axis=0, keepdims=True)
    lead_delta = jnp.sum(delta, axis=0, keepdims=True) * lead_inv

    def lead_grad(i, dq_t):
        weights = lead_ref[chunk_rows(i), 0:BLK] * lead_inv
        d_weights = lead_ref[chunk_rows(i), BLK : 2 * BLK]
        d_low = (weights * (d_weights - lead_delta) * SCALE).astype(BF16)
        both = jnp.concatenate([d_low, weights.astype(BF16)], axis=1)
        terms = lax.dot_general(both, pair, NN, preferred_element_type=F32)
        acc_ref[pl.ds(i * CHUNK, CHUNK)] = terms.reshape(CHUNK, BLK, 2 * HD)
        keys = jnp.concatenate([kt_ref[i * CHUNK + t] for t in range(CHUNK)], axis=1)
        return dq_t + lax.dot_general(keys, d_low, NN, preferred_element_type=F32)

    lead_dq_ref[...] = lax.fori_loop(0, blocks // CHUNK, lead_grad, jnp.zeros((HD, BLK), F32))

    def scores_slots(b, side, slots, pair, peak):
        index = named_blocks(pat_ref, b)[1]
        rows = jnp.concatenate([kv_ref[index[s]] for s in slots], axis=0)
        both = lax.dot_general(rows, pair, NT, preferred_element_type=F32)
        span = pl.ds(slots[0] * BLK, len(slots) * BLK)
        s_refs[side][span, :] = both[:, 0:BLK]
        g_refs[side][span, :] = both[:, BLK : 2 * BLK]
        top = jnp.max(both[:, 0:BLK].reshape(len(slots) * BLK // 8, 8, BLK), axis=0)
        return top if peak is None else jnp.maximum(peak, top)

    def exp_slot(b, side, s, peak, sums):
        named = named_blocks(pat_ref, b)[0]
        kept = named[s] >= 0
        for t in range(s):
            kept = jnp.logical_and(kept, named[s] != named[t])
        floor = peak + jnp.where(kept, 0.0, jnp.inf).astype(F32)
        raised = jnp.exp2(s_refs[side][slot_rows(s), :] * SCALE2 - floor)
        s_refs[side][slot_rows(s), :] = raised
        product = raised * g_refs[side][slot_rows(s), :]
        return sums[0] + rows_sum(raised), sums[1] + rows_sum(product)

    def grads_slots(side, slots, pair, inv_total, inv_scaled, delta):
        span = pl.ds(slots[0] * BLK, len(slots) * BLK)
        raised = s_refs[side][span, :]
        d_low = (raised * inv_scaled * (g_refs[side][span, :] - delta)).astype(BF16)
        x_refs[side][span, :] = d_low
        both = jnp.concatenate([d_low, (raised * inv_total).astype(BF16)], axis=1)
        return lax.dot_general(both, pair, NN, preferred_element_type=F32)

    def query_product(b, side):
        index = named_blocks(pat_ref, b)[1]
        keys = jnp.concatenate([kt_ref[i] for i in index], axis=1)
        return lax.dot_general(keys, x_refs[side][...], NN, preferred_element_type=F32)

    def query_grad(b, dq_t, q_part):
        dq = dq_t.T.astype(BF16).astype(F32)
        q_raw = got_ref[b, 0:BLK, :].astype(F32)
        q_inv = inverse_rms(q_raw)
        q_hat = q_raw * q_inv
        scaled = q_gain * dq
        mean = jnp.mean(scaled * q_hat, axis=-1, keepdims=True)
        dq_ref[b] = (q_inv * (scaled - q_hat * mean)).astype(BF16)
        return q_part + rows_sum(dq * q_hat)

    def step(b, side, q_part, ahead=True, behind=True):
        peak = peak_ref[side, 0:1, :] * SCALE2
        sums = (zero8, zero8)
        pair = pair_of(b + 1) if ahead else None
        top = None
        dq_t = query_product(b - 1, 1 - side) if behind else None
        for slots in GROUPS:
            if ahead:
                top = scores_slots(b + 1, 1 - side, slots, pair, top)
            for s in slots:
                sums = exp_slot(b, side, s, peak, sums)
        if ahead:
            peak_ref[1 - side, 0:1, :] = jnp.max(top, axis=0, keepdims=True)
        inv_total = 1.0 / jnp.sum(sums[0], axis=0, keepdims=True)
        delta = jnp.sum(sums[1], axis=0, keepdims=True) * inv_total
        pair = pair_of(b)
        index = named_blocks(pat_ref, b)[1]
        for slots in KEY_GROUPS:
            terms = grads_slots(side, slots, pair, inv_total, inv_total * SCALE, delta)
            for n, s in enumerate(slots):
                acc_ref[index[s]] += terms[n * BLK : (n + 1) * BLK]
        return query_grad(b - 1, dq_t, q_part) if behind else q_part

    x0[...] = jnp.zeros_like(x0)
    pair = pair_of(1)
    top = None
    for slots in GROUPS:
        top = scores_slots(1, 1, slots, pair, top)
    peak_ref[1, 0:1, :] = jnp.max(top, axis=0, keepdims=True)

    def two_steps(i, q_part):
        q_part = step(2 * i + 1, 1, q_part)
        return step(2 * i + 2, 0, q_part)

    q_part = lax.fori_loop(0, blocks // 2 - 1, two_steps, zero8)
    q_part = step(blocks - 1, 1, q_part, ahead=False)
    q_part = query_grad(blocks - 1, query_product(blocks - 1, 1), q_part)
    q_part = query_grad(0, lead_dq_ref[...], q_part)
    dq_copy = pltpu.make_async_copy(dq_ref, send_any.at[:, pl.ds(0, BLK)], sem)
    dq_copy.start()

    def finish(j, k_part):
        for half, ref in ((0, keep_ref), (HALF, give_ref)):
            rows = pl.ds(half, HALF)
            ref[j, 0:HALF, :] = acc_ref[j, rows, 0:HD].astype(BF16)
            ref[j, HALF:BLK, :] = acc_ref[j, rows, HD : 2 * HD].astype(BF16)
        return k_part + rows_sum(acc_ref[j, :, 0:HD] * khat_ref[j])

    k_part = zero8
    step_blocks = blocks // OUTS
    out_copies = []
    for n in range(OUTS):
        k_part = lax.fori_loop(n * step_blocks, (n + 1) * step_blocks, finish, k_part, unroll=4)
        chunk = pl.ds(n * step_blocks, step_blocks)
        for ref, out, copy_sems in ((give_ref, give_any, give_sems), (keep_ref, keep_any, keep_sems)):
            out_copies.append(pltpu.make_async_copy(ref.at[chunk], out.at[chunk], copy_sems.at[n]))
            out_copies[-1].start()
    parts = jnp.concatenate(
        [
            jnp.sum(q_part, axis=0, keepdims=True),
            jnp.sum(k_part, axis=0, keepdims=True),
            jnp.zeros((PARTS - 2, HD), F32),
        ],
        axis=0,
    )
    for j in range(blocks):
        parts_ref[j] = parts
    dq_copy.wait()
    for copy in out_copies:
        copy.wait()


def merge_kernel(blocks, keep_any, got_ref, send_any, out_any, keep_ref, sum_ref, sems, out_sems):
    step = blocks // OUTS
    loads = []
    for n in range(OUTS):
        chunk = pl.ds(n * step, step)
        loads.append(pltpu.make_async_copy(keep_any.at[chunk], keep_ref.at[chunk], sems.at[n]))
        loads[-1].start()

    def one_block(j, carry):
        sum_ref[j] = (keep_ref[j].astype(F32) + got_ref[j].astype(F32)).astype(BF16)
        return carry

    outs = []
    for n in range(OUTS):
        loads[n].wait()
        lax.fori_loop(n * step, (n + 1) * step, one_block, 0, unroll=4)
        chunk = pl.ds(n * step, step)
        outs.append(
            pltpu.make_async_copy(sum_ref.at[chunk], out_any.at[chunk, pl.ds(BLK, BLK)], out_sems.at[n])
        )
        outs[-1].start()
    for copy in outs:
        copy.wait()


def parts_sum_kernel(in_ref, out_ref):
    out_ref[...] = jnp.sum(in_ref[...], axis=0)[0:2]


def final_kernel(heads, in_ref, k_ref, gains_ref, q_grad_any, k_grad_ref, v_grad_ref, sems):
    copies = [
        pltpu.make_async_copy(in_ref.at[h, pl.ds(0, BLK)], q_grad_any.at[0, :, pl.ds(h * HD, HD)], sems.at[h])
        for h in range(heads)
    ]
    for copy in copies:
        copy.start()
    k_gain = gains_ref[1:2, :]
    for g in range(heads // 4):
        for core in range(2):
            first, second = 4 * g + core, 4 * g + 2 + core
            rows = pl.ds(core * HALF, HALF)
            cols = pl.ds(g * HD, HD)
            both = in_ref[first, BLK : 2 * BLK, :].astype(F32) + in_ref[second, BLK : 2 * BLK, :].astype(F32)
            v_grad_ref[0, rows, cols] = both[HALF:BLK].astype(BF16)
            values = k_ref[0, rows, cols].astype(F32)
            inverse = inverse_rms(values)
            scaled = k_gain * both[0:HALF].astype(BF16).astype(F32)
            total = jnp.sum(scaled * values, axis=-1, keepdims=True)
            grad = inverse * scaled - inverse * inverse * inverse * values * total / HD
            k_grad_ref[0, rows, cols] = grad.astype(BF16)
    for copy in copies:
        copy.wait()


def dp_step(values, step, dp_count):
    if step >= dp_count:
        return values
    return values + lax.ppermute(values, "dp", [(z, z ^ step) for z in range(dp_count)])


def struct(shape, dtype):
    return jax.ShapeDtypeStruct(shape, dtype)


def call(kernel, ins, outs, scratch=(), mib=12, aliases={}):
    return pl.pallas_call(
        kernel,
        out_shape=tuple(array for array, spec in outs),
        in_specs=list(ins),
        out_specs=tuple(spec for array, spec in outs),
        scratch_shapes=list(scratch),
        input_output_aliases=aliases,
        compiler_params=pltpu.CompilerParams(vmem_limit_bytes=mib << 20),
    )


def shards(heads, dp_count, q_raw, k_raw, v_raw, q_gain, k_gain, key_blocks, d_context):
    blocks = heads
    swap = [(s, s ^ 1) for s in range(heads)]
    mine = lax.broadcasted_iota(jnp.int32, (2, HD), 1) // (HD // dp_count) == lax.axis_index("dp")
    spread = jnp.concatenate([jnp.tile(q_gain, dp_count)[None], jnp.tile(k_gain, dp_count)[None]], axis=0)
    gains = jnp.where(mine, spread, 0.0)

    (sent,) = call(
        functools.partial(pack_kernel, heads),
        [HBM_SPEC] * 4,
        [(pltpu.HBM((heads, 3 * BLK, HD), BF16), HBM_SPEC)],
        [
            pltpu.VMEM(q_raw.shape[1:], BF16),
            pltpu.VMEM(d_context.shape[1:], BF16),
            pltpu.VMEM(k_raw.shape[1:], BF16),
            pltpu.VMEM(v_raw.shape[1:], BF16),
            pltpu.VMEM((heads, 3 * BLK, HD), BF16),
            pltpu.SemaphoreType.DMA((4 * PACKS,)),
            pltpu.SemaphoreType.DMA((PACKS,)),
        ],
    )(*[pltpu.with_memory_space_constraint(x, pltpu.HBM) for x in (q_raw, d_context, k_raw, v_raw)])
    arrived = lax.all_to_all(sent, "seq", 0, 0, tiled=True)
    for step in (8, 4, 2, 1):
        gains = dp_step(gains, step, dp_count)
    arrived, gains = lax.optimization_barrier((arrived, gains))
    other = lax.ppermute(arrived[:, 2 * BLK :], "seq", swap)

    send, keep, give, parts = call(
        functools.partial(attend_kernel, blocks),
        [SMEM_SPEC] + [VMEM_SPEC] * 2 + [HBM_SPEC],
        [
            (pltpu.HBM((blocks, 2 * BLK, HD), BF16), HBM_SPEC),
            (pltpu.HBM((blocks, BLK, HD), BF16), HBM_SPEC),
            (pltpu.HBM((blocks, BLK, HD), BF16), HBM_SPEC),
            (struct((blocks, PARTS, HD), F32), VMEM_SPEC),
        ],
        [
            pltpu.VMEM((blocks, BLK, HD), BF16),
            pltpu.VMEM((blocks, BLK, HD), BF16),
            pltpu.VMEM((blocks, BLK, HD), BF16),
            pltpu.VMEM((blocks, BLK, HD), BF16),
            pltpu.VMEM((blocks, BLK, 2 * HD), F32),
            pltpu.VMEM((blocks * BLK, 2 * BLK), F32),
            pltpu.VMEM((HD, BLK), F32),
            pltpu.VMEM((blocks, BLK, 2 * HD), BF16),
            pltpu.VMEM((blocks, HD, BLK), BF16),
            pltpu.VMEM((blocks, BLK, HD), F32),
            pltpu.VMEM((blocks, BLK, HD), BF16),
        ]
        + [pltpu.VMEM((SLOTS * BLK, BLK), F32)] * 4
        + [pltpu.VMEM((SLOTS * BLK, BLK), BF16)] * 2
        + [pltpu.VMEM((2, 8, BLK), F32)]
        + [pltpu.SemaphoreType.DMA] * 2
        + [pltpu.SemaphoreType.DMA((OUTS,))] * 2,
        mib=40,
    )(key_blocks, gains, arrived, pltpu.with_memory_space_constraint(other, pltpu.HBM))

    parts = lax.all_to_all(parts, "seq", 0, 0, tiled=True)
    got = lax.ppermute(give, "seq", swap)
    (send,) = call(
        functools.partial(merge_kernel, blocks),
        [HBM_SPEC, VMEM_SPEC, HBM_SPEC],
        [(pltpu.HBM(send.shape, BF16), HBM_SPEC)],
        [pltpu.VMEM((blocks, BLK, HD), BF16)] * 2 + [pltpu.SemaphoreType.DMA((OUTS,))] * 2,
        aliases={2: 0},
    )(pltpu.with_memory_space_constraint(keep, pltpu.HBM), got, send)
    back = lax.all_to_all(send, "seq", 0, 0, tiled=True)

    (totals,) = call(parts_sum_kernel, [VMEM_SPEC], [(struct((2, HD), F32), VMEM_SPEC)])(parts)
    totals = dp_step(totals, 1, dp_count)
    for step in (8, 4):
        totals = dp_step(totals, step, dp_count)
    totals = dp_step(totals, 2, dp_count)
    width = q_gain.shape[0]
    totals = lax.dynamic_slice_in_dim(totals, lax.axis_index("dp") * width, width, axis=1)

    q_grad, k_grad, v_grad = call(
        functools.partial(final_kernel, heads),
        [VMEM_SPEC] * 3,
        [
            (struct(q_raw.shape, BF16), HBM_SPEC),
            (struct(k_raw.shape, BF16), VMEM_SPEC),
            (struct(v_raw.shape, BF16), VMEM_SPEC),
        ],
        [pltpu.SemaphoreType.DMA((heads,))],
    )(back, k_raw, gains)
    return (q_grad, k_grad, v_grad, totals[0], totals[1])


def solution(mesh):
    placed = (
        P("dp", "seq", None),
        P("dp", "seq", None),
        P("dp", "seq", None),
        P("dp"),
        P("dp"),
        P("seq", None, None),
        P("dp", "seq", None),
    )
    return jax.shard_map(
        functools.partial(shards, mesh.shape["seq"], mesh.shape["dp"]),
        mesh=mesh,
        in_specs=placed,
        out_specs=(
            P("dp", "seq", None),
            P("dp", "seq", None),
            P("dp", "seq", None),
            P("dp"),
            P("dp"),
        ),
        check_vma=False,
    )
```
